256 devices in a mesh: vel: 32 (over y, x, core), gy: 8 (over z).
Axes of the slice: x: 4, y: 4, z: 8, core: 2. Of those that a mesh axis runs over, the one named last changes fastest.
Arguments:
- distribution: float32 [13824, 2, 32, 128], P('vel', None, 'gy'), may hold values from 0.5 to 1.5
- body_mask: int32 [2, 32, 128], P(None, 'gy'), may hold values from 0 to 1, as said below
- inflow_flags: int32 [2, 32], replicated, may hold values 0 or 1
Outputs:
- advanced: float32 [13824, 2, 32, 128], P('vel', None, 'gy')
The draws below stay inside these ranges and needn't reach their ends.
Inputs may be any that keep to these rules, and one draw needn't show every extreme that they name: `body_mask`: the body is one ellipse per plane, the same centre in both planes; it never touches the grid's edges.
All inputs are finite; a program needn't handle non-finite values.
Results may differ from the reference program's by a relative error of at most 0.0003.
Values sent between devices are 32-bit elements; how exact they have to be, the bound alone decides.
No kernel may reach another device: no remote copies, remote signals or barrier semaphores. Data moves between devices by JAX's collectives and lax.ppermute only.
A program may use at most 64 MiB of HBM per device.

```python
import jax
import jax.numpy as jnp
from jax import lax

NV1 = 24
NV = 13824
NZ = 2
NX = 128
NY = 32
STEPS = 2


def draw_body_mask(key, part):
    subkeys = jax.random.split(jax.random.fold_in(key, 7), 4)
    centre_x = jax.random.randint(subkeys[0], (), NX // 4, NX // 2 + 1)
    centre_y = jax.random.randint(subkeys[1], (), NY // 4, 3 * NY // 4 + 1)
    radius_x = jax.random.randint(subkeys[2], (), NX // 16 + 1, NX // 8 + 2)
    radius_y = jax.random.randint(subkeys[3], (), NY // 16 + 1, NY // 8 + 2)
    plane_index = jnp.arange(NZ, dtype=jnp.int32)[:, None, None]
    row_index = jnp.arange(NY, dtype=jnp.int32)[None, :, None]
    column = jnp.arange(NX, dtype=jnp.int32)[None, None, :]
    reach_x = radius_x + plane_index
    offset_x = column - centre_x
    offset_y = row_index - centre_y
    inside = offset_x * offset_x * radius_y * radius_y + offset_y * offset_y * reach_x * reach_x <= reach_x * reach_x * radius_y * radius_y
    return inside.astype(jnp.int32)


def plant(values, rng, least, high):
    index_at = [jax.random.randint(jax.random.fold_in(rng, axis), (), 0, length) for axis, length in enumerate(values.shape)]
    widest = values.shape.index(max(values.shape))
    next_to = index_at[:widest] + [(index_at[widest] + 1) % values.shape[widest]] + index_at[widest + 1:]
    return values.at[tuple(index_at)].set(least).at[tuple(next_to)].set(high)


def level_of(key, shape, cuts, least, high):
    factor_of = 1.0
    for position, blocks in cuts:
        heights = jax.random.uniform(jax.random.fold_in(jax.random.fold_in(key, 6), position), (blocks,), jnp.float32, least / len(cuts), high / len(cuts))
        factor_of = factor_of * jnp.repeat(jnp.exp(heights), shape[position] // blocks).reshape((-1,) + (1,) * (len(shape) - 1 - position))
    return factor_of


def setup_inputs(seed: int = 0) -> dict:
    streams_of = jax.random.split(jax.random.key(seed), 4)
    distribution = jnp.clip(0.5 + 1.0 * jax.random.uniform(streams_of[0], (NV, NZ, NY, NX), jnp.float32) ** level_of(streams_of[0], (NV, NZ, NY, NX), ((0, 32), (2, 8)), -0.2, 0.2), 0.5, 1.5)
    body_mask = draw_body_mask(jax.random.fold_in(streams_of[3], 71), 0)
    inflow_flags = plant((jax.random.randint(streams_of[2], (NZ, NY), 0, 4) < 3).astype(jnp.int32), jax.random.fold_in(streams_of[2], 1), 0, 1)
    return {"distribution": distribution, "body_mask": body_mask, "inflow_flags": inflow_flags}


dv_step = 0.6
time_step = 0.25
diffusivity_ratio = 2.0 / 3.0
baseline_shear_coefficient = 3000.0
baseline_warmth = 3.0
shear_power_index = 0.81
free_density = 200.0
free_temp = 1.0
free_speed = 3.0
wall_density = 200.0
wall_temp = 1.5


def velocity_grid(per_axis, first_index, length):
    velocity_index = first_index + jnp.arange(length, dtype=jnp.int32)
    index_x = velocity_index // (per_axis * per_axis)
    index_y = (velocity_index // per_axis) % per_axis
    index_z = velocity_index % per_axis
    centre_index = 0.5 * (per_axis - 1)
    grid_x = (index_x.astype(jnp.float32) - centre_index) * dv_step
    grid_y = (index_y.astype(jnp.float32) - centre_index) * dv_step
    grid_z = (index_z.astype(jnp.float32) - centre_index) * dv_step
    return grid_x, grid_y, grid_z


def gaussian_distribution(fluid_concentration, cell_kinetic_warmth, random_motion_first, random_motion_second, random_motion_third):
    magnitude_square_norm = random_motion_first * random_motion_first + random_motion_second * random_motion_second + random_motion_third * random_motion_third
    return fluid_concentration / jnp.power(2.0 * jnp.pi * cell_kinetic_warmth, 1.5) * jnp.exp(-magnitude_square_norm / (2.0 * cell_kinetic_warmth))


def beam_warming(centre, upwind_one, upwind_two, courant):
    return (centre - 0.5 * courant * (3.0 * centre - 4.0 * upwind_one + upwind_two)
            + 0.5 * courant * courant * (centre - 2.0 * upwind_one + upwind_two))


def sweep_x(state_now, velocity_x, inflow_value, flag_rows):
    x_cells = state_now.shape[-1]
    right_ghost = state_now[..., x_cells - 1:]
    left_ghost = jnp.where(flag_rows[..., None] > 0, inflow_value, state_now[..., :1])
    padded = jnp.concatenate([left_ghost, left_ghost, state_now, right_ghost, right_ghost], -1)
    courant = jnp.abs(velocity_x) * time_step
    forward = beam_warming(state_now, padded[..., 1:x_cells + 1], padded[..., 0:x_cells], courant)
    backward = beam_warming(state_now, padded[..., 3:x_cells + 3], padded[..., 4:x_cells + 4], courant)
    return jnp.where(velocity_x > 0, forward, backward)


def sweep_y(padded, velocity_y):
    row_count = padded.shape[-2] - 4
    centre = padded[..., 2:row_count + 2, :]
    courant = jnp.abs(velocity_y) * time_step
    forward = beam_warming(centre, padded[..., 1:row_count + 1, :], padded[..., 0:row_count, :], courant)
    backward = beam_warming(centre, padded[..., 3:row_count + 3, :], padded[..., 4:row_count + 4, :], courant)
    return jnp.where(velocity_y > 0, forward, backward)


def drift_of(first_sums):
    fluid_concentration = first_sums[0]
    return fluid_concentration, first_sums[1] / fluid_concentration, first_sums[2] / fluid_concentration, first_sums[3] / fluid_concentration


def second_terms(values, grid_x, grid_y, grid_z, drift_x, drift_y, drift_z):
    random_motion_first = grid_x - drift_x[None]
    random_motion_second = grid_y - drift_y[None]
    random_motion_third = grid_z - drift_z[None]
    magnitude_square_norm = random_motion_first * random_motion_first + random_motion_second * random_motion_second + random_motion_third * random_motion_third
    weighted = (dv_step ** 3) * values * magnitude_square_norm
    return jnp.stack([jnp.sum(weighted, 0) / 3.0, 0.5 * jnp.sum(random_motion_first * weighted, 0),
                      0.5 * jnp.sum(random_motion_second * weighted, 0), 0.5 * jnp.sum(random_motion_third * weighted, 0)])


def relax(values, grid_x, grid_y, grid_z, fluid_concentration, drift_x, drift_y, drift_z, second):
    isotropic_stress = second[0]
    cell_kinetic_warmth = isotropic_stress / fluid_concentration
    random_motion_first = grid_x - drift_x[None]
    random_motion_second = grid_y - drift_y[None]
    random_motion_third = grid_z - drift_z[None]
    magnitude_square_norm = random_motion_first * random_motion_first + random_motion_second * random_motion_second + random_motion_third * random_motion_third
    target_distribution = gaussian_distribution(fluid_concentration[None], cell_kinetic_warmth[None], random_motion_first, random_motion_second, random_motion_third)
    energy_current_projection = random_motion_first * second[1][None] + random_motion_second * second[2][None] + random_motion_third * second[3][None]
    skewness_adjustment = target_distribution * (1.0 + (1.0 - diffusivity_ratio) * energy_current_projection / (5.0 * isotropic_stress * cell_kinetic_warmth)[None]
                             * (magnitude_square_norm / cell_kinetic_warmth[None] - 5.0))
    relaxation_rate = isotropic_stress / (baseline_shear_coefficient * jnp.power(cell_kinetic_warmth / baseline_warmth, shear_power_index))
    damping = jnp.exp(-relaxation_rate * time_step)
    return skewness_adjustment + (values - skewness_adjustment) * damping[None]


def moment_table(grid_x, grid_y, grid_z):
    weights = jnp.full(grid_x.shape, dv_step ** 3, jnp.float32)
    return jnp.stack([weights, weights * grid_x, weights * grid_y, weights * grid_z])


def reference(distribution, body_mask, inflow_flags):
    speed_x, speed_y, speed_z = velocity_grid(NV1, 0, NV)
    inflow = gaussian_distribution(free_density, free_temp, speed_x - free_speed, speed_y, speed_z)
    wall = gaussian_distribution(wall_density, wall_temp, speed_x, speed_y, speed_z)
    table = moment_table(speed_x, speed_y, speed_z)
    columns_x, columns_y, columns_z = speed_x[:, None], speed_y[:, None], speed_z[:, None]

    def transport(items):
        plane_state, velocity_x, velocity_y, inflow_value = items
        swept = sweep_x(plane_state, velocity_x, inflow_value, inflow_flags)
        padded = jnp.concatenate([swept[:, NY - 2:, :], swept, swept[:, :2, :]], 1)
        return sweep_y(padded, velocity_y)

    def collide(values):
        fluid_concentration, drift_x, drift_y, drift_z = drift_of(jnp.dot(table, values, precision=lax.Precision.HIGHEST))
        second = second_terms(values, columns_x, columns_y, columns_z, drift_x, drift_y, drift_z)
        return relax(values, columns_x, columns_y, columns_z, fluid_concentration, drift_x, drift_y, drift_z, second)

    state_now = distribution
    for step_index in range(STEPS):
        moved = lax.map(transport, (state_now, speed_x, speed_y, inflow))
        blocks = moved.reshape(NV, NZ * NY // 8, 8 * NX).transpose(1, 0, 2)
        blocks = lax.map(collide, blocks)
        relaxed = blocks.transpose(1, 0, 2).reshape(NV, NZ, NY, NX)
        state_now = jnp.where(body_mask[None] > 0, wall[:, None, None, None], relaxed)
    return state_now
```

```python
import math

import jax
import jax.numpy as jnp
from jax import lax
from jax.experimental import pallas as pl
from jax.experimental.pallas import tpu as pltpu
from jax.sharding import PartitionSpec as P

NV1 = 24
NB = 18
HALF = NV1 // 2
NMOM = 13
STEP = 0.6
DT = 0.25
WEIGHT = STEP**3
CENTRE = 0.5 * (NV1 - 1)
ZS = [(c - CENTRE) * STEP for c in range(NV1)]
INFLOW_Z = [math.exp(-0.5 * z * z) for z in ZS]
INFLOW_SUMS = [sum(z**k * g for z, g in zip(ZS, INFLOW_Z)) for k in range(4)]
INFLOW_SCALE = 200.0 / (2.0 * math.pi) ** 1.5
SHAPE = (8, 128)
F32 = jnp.float32


def iotas():
    rows = lax.rem(lax.broadcasted_iota(jnp.int32, SHAPE, 0), 4)
    lanes = lax.broadcasted_iota(jnp.int32, SHAPE, 1)
    return rows, lanes


def flag_tile(flags_ref, gy):
    subs = lax.broadcasted_iota(jnp.int32, SHAPE, 0)
    tile = jnp.zeros(SHAPE, jnp.int32)
    for plane in range(2):
        for row in range(4):
            tile = jnp.where(subs == plane * 4 + row, flags_ref[plane, gy * 4 + row], tile)
    return tile


def weights_of(speed):
    k = jnp.abs(speed) * DT
    return 1.0 - 1.5 * k + 0.5 * k * k, 2.0 * k - k * k, 0.5 * k * k - 0.5 * k


def block_speeds(vel, block):
    index = vel * NB + block
    a = lax.div(index, NV1)
    b = index - a * NV1
    return (a.astype(F32) - CENTRE) * STEP, (b.astype(F32) - CENTRE) * STEP, b


def inflow_block(speed_x, speed_y):
    drift = speed_x - 3.0
    return INFLOW_SCALE * jnp.exp(jnp.full(SHAPE, -0.5 * (drift * drift + speed_y * speed_y), F32))


def sweep(values, ghost, coef, shift, edge, inflow_edge):
    one = pltpu.roll(values, shift, 1)
    one = jnp.where(inflow_edge, ghost, jnp.where(edge, values, one))
    two = jnp.where(edge, one, pltpu.roll(one, shift, 1))
    return coef[0] * values + coef[1] * one + coef[2] * two


def side_masks(rows, up):
    far = jnp.where(up, 3, 0)
    near = jnp.where(up, 0, 3)
    first = rows == far
    last = rows == near
    low = rows < 2
    tail = low != up
    return first, tail, last, jnp.logical_not(tail)


def add_moments(sums_ref, base, z, speed_x, speed_y):
    sq = speed_x * speed_x + speed_y * speed_y
    x0 = speed_x * z[0]
    y0 = speed_y * z[0]
    terms = [
        z[0], x0, y0, z[1],
        speed_x * x0, speed_y * y0, z[2],
        speed_x * y0, speed_x * z[1], speed_y * z[1],
        sq * x0 + speed_x * z[2], sq * y0 + speed_y * z[2], sq * z[1] + z[3],
    ]
    for m, term in enumerate(terms):
        sums_ref[base + m] = sums_ref[base + m] + term


def block_moments(sums_ref, z, speed_x, speed_y, inflow, coef_x, shift_x, edge, inflow_edge, up, rows):
    first, tail, last, head = side_masks(rows, up)
    c0, c1, c2 = weights_of(speed_y)
    zero = jnp.zeros(SHAPE, F32)
    c1v = jnp.full(SHAPE, c1, F32)
    c2v = jnp.full(SHAPE, c2, F32)
    own1, cross1 = jnp.where(last, zero, c1v), jnp.where(last, c1v, zero)
    own2, cross2 = jnp.where(head, zero, c2v), jnp.where(head, c2v, zero)
    s1 = jnp.where(up, 1, 7)
    s2 = jnp.where(up, 2, 6)
    own, cross = [], []
    for k in range(4):
        swept = sweep(z[k], INFLOW_SUMS[k] * inflow, coef_x, shift_x, edge, inflow_edge)
        r1 = pltpu.roll(swept, s1, 0)
        r2 = pltpu.roll(swept, s2, 0)
        own.append(c0 * swept + own1 * r1 + own2 * r2)
        cross.append(cross1 * r1 + cross2 * r2)
    add_moments(sums_ref, 0, own, speed_x, speed_y)
    add_moments(sums_ref, NMOM, cross, speed_x, speed_y)


def swap_planes(sums_ref):
    for m in range(NMOM, 2 * NMOM):
        sums_ref[m] = pltpu.roll(sums_ref[m], 4, 0)


def z_sums(z, low, high, c):
    s = low + high
    d = high - low
    speed = ZS[NV1 - 1 - c]
    z0, z1, z2, z3 = z
    return [z0 + s, z1 + speed * d, z2 + speed**2 * s, z3 + speed**3 * d]


def pack(low, high, tail, s2b):
    return jnp.where(tail, pltpu.roll(low, 4, 0), pltpu.roll(high, s2b, 0))


def first_kernel(flags_ref, f_hbm, sums_ref, halo_ref, f_ref, sems):
    for j in range(NB):
        pltpu.make_async_copy(f_hbm.at[pl.ds(NV1 * j, NV1)], f_ref.at[pl.ds(NV1 * j, NV1)], sems.at[j]).start()
    vel, gy = lax.axis_index("vel"), lax.axis_index("gy")
    rows, lanes = iotas()
    right = vel >= 16
    shift_x = jnp.where(right, 1, 127)
    edge = lanes == jnp.where(right, 0, 127)
    own_flags = jnp.where(right, flag_tile(flags_ref, gy), 0)
    inflow_edge = jnp.logical_and(edge, own_flags > 0)
    for m in range(2 * NMOM):
        sums_ref[m] = jnp.zeros(SHAPE, F32)

    def body(j, carry):
        speed_x, speed_y, b = block_speeds(vel, j)
        up = b >= HALF
        first, tail, last, head = side_masks(rows, up)
        s2b = jnp.where(up, 6, 2)
        pltpu.make_async_copy(f_hbm.at[pl.ds(NV1 * j, NV1)], f_ref.at[pl.ds(NV1 * j, NV1)], sems.at[j]).wait()
        z = [jnp.zeros(SHAPE, F32)] * 4
        for c in range(HALF):
            low = f_ref[NV1 * j + c]
            high = f_ref[NV1 * j + (NV1 - 1 - c)]
            z = z_sums(z, low, high, c)
            halo_ref[HALF * j + c] = pack(low, high, tail, s2b)
        z = [WEIGHT * v for v in z]
        inflow = WEIGHT * inflow_block(speed_x, speed_y)
        block_moments(sums_ref, z, speed_x, speed_y, inflow, weights_of(speed_x), shift_x, edge, inflow_edge, up, rows)
        return carry

    lax.fori_loop(0, NB, body, 0)
    swap_planes(sums_ref)


def cell_values(mom, solid):
    n = mom[0]
    inv = 1.0 / n
    ux, uy, uz = mom[1] * inv, mom[2] * inv, mom[3] * inv
    xx, yy, zz, xy, xz, yz = mom[4:10]
    energy = xx + yy + zz
    usq = ux * ux + uy * uy + uz * uz
    p = (energy - n * usq) * (1.0 / 3.0)
    common = 2.0 * n * usq - energy
    qx = 0.5 * (mom[10] - 2.0 * (xx * ux + xy * uy + xz * uz) + common * ux)
    qy = 0.5 * (mom[11] - 2.0 * (xy * ux + yy * uy + yz * uz) + common * uy)
    qz = 0.5 * (mom[12] - 2.0 * (xz * ux + yz * uy + zz * uz) + common * uz)
    temp = p * inv
    rate = p / (3000.0 * jnp.exp(0.81 * jnp.log(temp * (1.0 / 3.0))))
    damp = jnp.exp(-DT * rate)
    skew = (1.0 / 15.0) / (p * temp)
    zero = jnp.zeros(SHAPE, F32)
    n = jnp.where(solid, 200.0, n)
    temp = jnp.where(solid, 1.5, temp)
    damp = jnp.where(solid, zero, damp)
    skew = jnp.where(solid, zero, skew)
    ux, uy, uz = (jnp.where(solid, zero, u) for u in (ux, uy, uz))
    wide = 2.0 * math.pi * temp
    scale = n / (wide * jnp.sqrt(wide)) * (1.0 - damp)
    return scale, ux, uy, uz, 1.0 / temp, skew * qx, skew * qy, skew * qz, damp


def step_kernel(last_step, flags_ref, mask_ref, mom_ref, f_hbm, halo_hbm, *refs):
    if last_step:
        out_hbm, f_ref, in_ref, o_ref, z_ref, sems, hsems, osems = refs
    else:
        out_hbm, sums_ref, halo_out, f_ref, in_ref, o_ref, z_ref, sems, hsems, osems = refs

    def f_copy(j):
        return pltpu.make_async_copy(f_hbm.at[pl.ds(NV1 * j, NV1)], f_ref.at[pl.ds(NV1 * j, NV1)], sems.at[j])

    def h_copy(j):
        return pltpu.make_async_copy(halo_hbm.at[pl.ds(HALF * j, HALF)], in_ref.at[pl.ds(HALF * j, HALF)], hsems.at[j])

    def o_copy(j):
        return pltpu.make_async_copy(o_ref.at[pl.ds(NV1 * j, NV1)], out_hbm.at[pl.ds(NV1 * j, NV1)], osems.at[j])

    for j in range(NB):
        f_copy(j).start()
        h_copy(j).start()
    vel, gy = lax.axis_index("vel"), lax.axis_index("gy")
    rows, lanes = iotas()
    right = vel >= 16
    shift_x = jnp.where(right, 1, 127)
    edge = lanes == jnp.where(right, 0, 127)
    own_flags = jnp.where(right, flag_tile(flags_ref, gy), 0)
    low_flags = jnp.where(right, flag_tile(flags_ref, lax.rem(gy + 7, 8)), 0)
    high_flags = jnp.where(right, flag_tile(flags_ref, lax.rem(gy + 1, 8)), 0)
    inflow_edge = jnp.logical_and(edge, own_flags > 0)
    solid = mask_ref[...] > 0
    scale, ux, uy, uz, inv_t, qx, qy, qz, damp = cell_values([mom_ref[m] for m in range(NMOM)], solid)
    half_inv = -0.5 * inv_t
    for c in range(NV1):
        cz = ZS[c] - uz
        sq = cz * cz
        z_ref[c] = jnp.exp(sq * half_inv)
        z_ref[NV1 + c] = cz * qz
        z_ref[2 * NV1 + c] = sq * inv_t
    if not last_step:
        for m in range(2 * NMOM):
            sums_ref[m] = jnp.zeros(SHAPE, F32)

    def body(j, carry):
        speed_x, speed_y, b = block_speeds(vel, j)
        up = b >= HALF
        first, tail, last, head = side_masks(rows, up)
        s1 = jnp.where(up, 1, 7)
        s2 = jnp.where(up, 2, 6)
        s1b = jnp.where(up, 7, 1)
        s2b = jnp.where(up, 6, 2)
        flags = jnp.where(up, low_flags, high_flags)
        halo_flags = jnp.where(tail, pltpu.roll(flags, 4, 0), pltpu.roll(flags, s2b, 0))
        halo_edge = jnp.logical_and(edge, halo_flags > 0)
        coef_x = weights_of(speed_x)
        y0, y1, y2 = weights_of(speed_y)
        d0, d1, d2 = damp * y0, damp * y1, damp * y2
        cx, cy = speed_x - ux, speed_y - uy
        sq = cx * cx + cy * cy
        e_xy = scale * jnp.exp(sq * half_inv)
        q_xy = cx * qx + cy * qy
        s_xy = sq * inv_t - 5.0
        inflow = inflow_block(speed_x, speed_y)
        f_copy(j).wait()
        h_copy(j).wait()

        def relax(c, swept, one, two):
            target = e_xy * z_ref[c]
            shape = (q_xy + z_ref[NV1 + c]) * (s_xy + z_ref[2 * NV1 + c])
            return d0 * swept + d1 * one + d2 * two + (target + target * shape)

        z = [jnp.zeros(SHAPE, F32)] * 4
        for c in range(HALF):
            h = NV1 - 1 - c
            ghost = INFLOW_Z[c] * inflow
            low = sweep(f_ref[NV1 * j + c], ghost, coef_x, shift_x, edge, inflow_edge)
            high = sweep(f_ref[NV1 * j + h], ghost, coef_x, shift_x, edge, inflow_edge)
            halo = sweep(in_ref[HALF * j + c], ghost, coef_x, shift_x, edge, halo_edge)
            low1 = pltpu.roll(jnp.where(first, halo, low), s1, 0)
            low2 = pltpu.roll(jnp.where(tail, halo, low), s2, 0)
            high1 = jnp.where(last, pltpu.roll(halo, s1b, 0), pltpu.roll(high, s1, 0))
            high2 = jnp.where(head, halo, pltpu.roll(high, s2, 0))
            low = relax(c, low, low1, low2)
            high = relax(h, high, high1, high2)
            o_ref[NV1 * j + c] = low
            o_ref[NV1 * j + h] = high
            if not last_step:
                z = z_sums(z, low, high, c)
                halo_out[HALF * j + c] = pack(low, high, tail, s2b)
        o_copy(j).start()
        if not last_step:
            z = [WEIGHT * v for v in z]
            block_moments(
                sums_ref, z, speed_x, speed_y, WEIGHT * inflow, coef_x, shift_x, edge, inflow_edge, up, rows
            )
        return carry

    lax.fori_loop(0, NB, body, 0)
    if not last_step:
        swap_planes(sums_ref)
    for j in range(NB):
        o_copy(j).wait()


def any_spec():
    return pl.BlockSpec(memory_space=pl.ANY)


def smem_spec():
    return pl.BlockSpec(memory_space=pltpu.SMEM)


def vmem_spec():
    return pl.BlockSpec(memory_space=pltpu.VMEM)


SUMS = jax.ShapeDtypeStruct((2 * NMOM, 8, 128), F32)
HALO = jax.ShapeDtypeStruct((NB * HALF, 8, 128), F32)
STATE = jax.ShapeDtypeStruct((NB * NV1, 8, 128), F32)
DMAS = pltpu.SemaphoreType.DMA((NB,))


def first_call(flags, f):
    return pl.pallas_call(
        first_kernel,
        out_shape=(SUMS, HALO),
        in_specs=[smem_spec(), any_spec()],
        out_specs=(vmem_spec(), vmem_spec()),
        scratch_shapes=[pltpu.VMEM(STATE.shape, F32), DMAS],
        name="first",
    )(flags, f)


def step_call(last_step, flags, mask, mom, f, halo):
    def kernel(*refs):
        step_kernel(last_step, *refs)

    scratch = [
        pltpu.VMEM(STATE.shape, F32),
        pltpu.VMEM(HALO.shape, F32),
        pltpu.VMEM(STATE.shape, F32),
        pltpu.VMEM((3 * NV1, 8, 128), F32),
        DMAS,
        DMAS,
        DMAS,
    ]
    return pl.pallas_call(
        kernel,
        out_shape=(STATE,) if last_step else (STATE, SUMS, HALO),
        in_specs=[smem_spec(), vmem_spec(), vmem_spec(), any_spec(), any_spec()],
        out_specs=(any_spec(),) if last_step else (any_spec(), vmem_spec(), vmem_spec()),
        scratch_shapes=scratch,
        name="last" if last_step else "middle",
    )(flags, mask, mom, f, halo)


def upwind(vel, group):
    return 1 if (NB * vel + 6 * group) % NV1 >= HALF else -1


def bulk_halo(halo):
    parts = []
    for group in range(3):
        pairs = [
            (v * 8 + g, v * 8 + (g + upwind(v, group)) % 8) for v in range(32) for g in range(8)
        ]
        parts.append(lax.ppermute(halo[72 * group : 72 * group + 72], ("vel", "gy"), pairs))
    return jnp.concatenate(parts)


def exchange(values, dy, dx, dc):
    pairs = []
    for v in range(32):
        y, x, c = v // 8, v // 2 % 4, v % 2
        pairs.append((v, (y ^ dy) * 8 + (x ^ dx) * 2 + (c ^ dc)))
    return lax.ppermute(values, "vel", pairs)


def total_moments(sums):
    own, cross = sums[:NMOM], sums[NMOM:]
    up = lax.ppermute(cross, "gy", [(g, (g + 1) % 8) for g in range(8)])
    down = lax.ppermute(cross, "gy", [((g + 1) % 8, g) for g in range(8)])
    rows = lax.broadcasted_iota(jnp.int32, (1, 8, 1), 1) % 4
    mom = own + jnp.where(rows < 2, up, down)
    for dy, dx, dc in ((0, 0, 1), (0, 1, 0), (0, 3, 0), (1, 0, 0), (3, 0, 0)):
        mom = mom + exchange(mom, dy, dx, dc)
    return mom


def shards(distribution, body_mask, inflow_flags):
    f = distribution.reshape(NB * NV1, 8, 128)
    mask = body_mask.reshape(8, 128)
    sums, halo = first_call(inflow_flags, f)
    mom = total_moments(sums)
    halo = bulk_halo(halo)
    f, sums, halo = step_call(False, inflow_flags, mask, mom, f, halo)
    mom = total_moments(sums)
    halo = bulk_halo(halo)
    (f,) = step_call(True, inflow_flags, mask, mom, f, halo)
    return f.reshape(distribution.shape)


def solution(mesh):
    placed = (P("vel", None, "gy", None), P(None, "gy", None), P())
    return jax.shard_map(
        shards, mesh=mesh, in_specs=placed, out_specs=P("vel", None, "gy", None), check_vma=False
    )
```

```python
import math

import jax
import jax.numpy as jnp
from jax import lax
from jax.experimental import pallas as pl
from jax.experimental.pallas import tpu as pltpu
from jax.sharding import PartitionSpec as P

NV1 = 24
NB = 18
HALF = NV1 // 2
NGROUP = 3
PER = NB // NGROUP
SLOT = PER * HALF
NMOM = 13
NPACK = 7
ORDERS = ((0, 0), (1, 0), (2, 0), (3, 0), (0, 1), (1, 1), (2, 1), (0, 2), (1, 2), (0, 3))
NORD = len(ORDERS)
STEP = 0.6
DT = 0.25
WEIGHT = STEP**3
CENTRE = 0.5 * (NV1 - 1)
ZS = [(c - CENTRE) * STEP for c in range(NV1)]
INFLOW_Z = [math.exp(-0.5 * z * z) for z in ZS]
INFLOW_SUMS = [sum(z**k * g for z, g in zip(ZS, INFLOW_Z)) for k in range(4)]
INFLOW_SCALE = 200.0 / (2.0 * math.pi) ** 1.5
SHAPE = (8, 128)
F32 = jnp.float32


def iotas():
    subs = lax.broadcasted_iota(jnp.int32, SHAPE, 0)
    lanes = lax.broadcasted_iota(jnp.int32, SHAPE, 1)
    return subs, jnp.bitwise_and(subs, 3), lanes


def flag_tile(flags_ref, subs, gy):
    tile = jnp.zeros(SHAPE, jnp.int32)
    for plane in range(2):
        for row in range(4):
            tile = jnp.where(subs == plane * 4 + row, flags_ref[plane, gy * 4 + row], tile)
    return tile > 0


def weights_of(speed):
    k = jnp.abs(speed) * DT
    return 1.0 - 1.5 * k + 0.5 * k * k, 2.0 * k - k * k, 0.5 * k * k - 0.5 * k


def speeds(vel, block):
    index = vel * NB + block
    a = lax.div(index, NV1)
    b = index - a * NV1
    return (a.astype(F32) - CENTRE) * STEP, (b.astype(F32) - CENTRE) * STEP


def group_state(vel, group):
    first = lax.rem(3 * vel, 4)

    def up_of(g):
        return lax.rem(first + g, 4) >= 2

    up = up_of(group)
    slot = jnp.where(jnp.logical_and(group > 0, up_of(0) == up), 1, 0)
    slot = slot + jnp.where(jnp.logical_and(group > 1, up_of(1) == up), 1, 0)
    a_slot = lax.div(vel * NB + PER * group, NV1) - lax.div(vel * NB, NV1)
    return up, slot, a_slot


def over_blocks(vel, body):
    for right in (True, False):

        @pl.when((vel >= 16) == right)
        def _(right=right):
            def group_loop(group, carry):
                up, slot, a_slot = group_state(vel, group)
                for up_now in (True, False):

                    @pl.when(up == up_now)
                    def _(up_now=up_now):
                        def block_loop(k, c):
                            body(PER * group + k, slot * SLOT + HALF * k, a_slot, right, up_now)
                            return c

                        lax.fori_loop(0, PER, block_loop, 0)

                return carry

            lax.fori_loop(0, NGROUP, group_loop, 0)


def inflow_block(speed_x, speed_y):
    drift = speed_x - 3.0
    return INFLOW_SCALE * jnp.exp(jnp.full(SHAPE, -0.5 * (drift * drift + speed_y * speed_y), F32))


def x_weights(speed_x, lanes, right, inflow_rows):
    c0, c1, c2 = weights_of(speed_x)
    zero = jnp.zeros(SHAPE, F32)
    v0, v1, v2 = (jnp.full(SHAPE, c, F32) for c in (c0, c1, c2))
    if right:
        edge, next_edge, inner = lanes == 0, lanes == 1, lanes >= 2
        held = jnp.logical_not(inflow_rows)
        a0 = jnp.where(jnp.logical_and(edge, held), 1.0, v0)
        a1 = jnp.where(edge, zero, jnp.where(jnp.logical_and(next_edge, held), v1 + v2, v1))
        a2 = jnp.where(inner, v2, zero)
        ghost = jnp.where(inflow_rows, jnp.where(edge, v1 + v2, jnp.where(next_edge, v2, zero)), zero)
        return a0, a1, a2, ghost
    edge, next_edge, inner = lanes == 127, lanes == 126, lanes < 126
    a0 = jnp.where(edge, 1.0, v0)
    a1 = jnp.where(edge, zero, jnp.where(next_edge, v1 + v2, v1))
    a2 = jnp.where(inner, v2, zero)
    return a0, a1, a2, None


def sweep_x(values, weights, right, ghost):
    one = pltpu.roll(values, 1 if right else 127, 1)
    two = pltpu.roll(values, 2 if right else 126, 1)
    swept = weights[0] * values + weights[1] * one + weights[2] * two
    return swept if ghost is None else swept + ghost


def z_sums(z, low, high, c):
    s = low + high
    d = high - low
    speed = ZS[NV1 - 1 - c]
    z0, z1, z2, z3 = z
    return [z0 + s, z1 + speed * d, z2 + speed**2 * s, z3 + speed**3 * d]


def pack_halo(low, high, rows, up):
    if up:
        return jnp.where(rows >= 2, pltpu.roll(low, 4, 0), pltpu.roll(high, 6, 0))
    return jnp.where(rows < 2, pltpu.roll(low, 4, 0), pltpu.roll(high, 2, 0))


def block_moments(acc_ref, a_slot, z, speed_x, speed_y, lanes, rows, right, up, inflow_rows):
    weights = x_weights(speed_x, lanes, right, inflow_rows)
    c0, c1, c2 = weights_of(speed_y)
    zero = jnp.zeros(SHAPE, F32)
    v1, v2 = jnp.full(SHAPE, c1, F32), jnp.full(SHAPE, c2, F32)
    last = rows == (0 if up else 3)
    head = rows < 2 if up else rows >= 2
    own1, cross1 = jnp.where(last, zero, v1), jnp.where(last, v1, zero)
    own2, cross2 = jnp.where(head, zero, v2), jnp.where(head, v2, zero)
    own, cross = [], []
    base = weights[3] * inflow_block(speed_x, speed_y) if right else None
    for k in range(4):
        ghost = INFLOW_SUMS[k] * base if right and k % 2 == 0 else None
        swept = sweep_x(z[k], weights, right, ghost)
        r1 = pltpu.roll(swept, 1 if up else 7, 0)
        r2 = pltpu.roll(swept, 2 if up else 6, 0)
        own.append(c0 * swept + own1 * r1 + own2 * r2)
        cross.append(cross1 * r1 + cross2 * r2)
    for side, values in enumerate((own, cross)):
        powers = {}
        for m, (j, k) in enumerate(ORDERS):
            powers[j, k] = values[k] if j == 0 else speed_y * powers[j - 1, k]
            at = a_slot * (2 * NORD) + side * NORD + m
            acc_ref[at] = acc_ref[at] + powers[j, k]


def clear_moments(acc_ref):
    for m in range(4 * NORD):
        acc_ref[m] = jnp.zeros(SHAPE, F32)


def finish_moments(acc_ref, keep_ref, send_ref, vel, rows):
    first_a = lax.div(vel * NB, NV1).astype(F32)
    odd = lax.rem(vel, 2) == 1
    low = rows < 2
    for side in range(2):
        total = None
        for a_slot in range(2):
            x = (first_a + (a_slot - CENTRE)) * STEP
            o = {jk: WEIGHT * acc_ref[a_slot * 2 * NORD + side * NORD + m] for m, jk in enumerate(ORDERS)}
            xo = x * o[0, 0]
            xx = x * xo
            terms = [
                o[0, 0], xo, o[1, 0], o[0, 1],
                xx, o[2, 0], o[0, 2],
                x * o[1, 0], x * o[0, 1], o[1, 1],
                x * xx + x * (o[2, 0] + o[0, 2]),
                x * x * o[1, 0] + (o[3, 0] + o[1, 2]),
                x * x * o[0, 1] + (o[2, 1] + o[0, 3]),
            ]
            total = terms if total is None else [p + q for p, q in zip(total, terms)]
        if side:
            total = [pltpu.roll(v, 4, 0) for v in total]
        for k in range(NPACK):
            one = total[k]
            two = total[k + NPACK] if k + NPACK < NMOM else one
            upper = jnp.where(low, one, pltpu.roll(two, 2, 0))
            lower = jnp.where(low, pltpu.roll(two, 6, 0), one)
            keep_ref[side * NPACK + k] = jnp.where(odd, lower, upper)
            send_ref[side * NPACK + k] = jnp.where(odd, upper, lower)


def first_kernel(flags_ref, f_hbm, f_ref, keep_ref, send_ref, up_ref, down_ref, acc_ref, sems):
    def f_copy(j):
        return pltpu.make_async_copy(f_hbm.at[pl.ds(NV1 * j, NV1)], f_ref.at[pl.ds(NV1 * j, NV1)], sems.at[j])

    for j in range(NB):
        f_copy(j).start()
    vel, gy = lax.axis_index("vel"), lax.axis_index("gy")
    subs, rows, lanes = iotas()
    inflow_rows = flag_tile(flags_ref, subs, gy)
    clear_moments(acc_ref)

    def body(j, at, a_slot, right, up):
        speed_x, speed_y = speeds(vel, j)
        out_ref = up_ref if up else down_ref
        f_copy(j).wait()
        z = [jnp.zeros(SHAPE, F32)] * 4
        for c in range(HALF):
            low = f_ref[NV1 * j + c]
            high = f_ref[NV1 * j + (NV1 - 1 - c)]
            z = z_sums(z, low, high, c)
            out_ref[at + c] = pack_halo(low, high, rows, up)
        block_moments(acc_ref, a_slot, z, speed_x, speed_y, lanes, rows, right, up, inflow_rows)

    over_blocks(vel, body)
    finish_moments(acc_ref, keep_ref, send_ref, vel, rows)


def move_kernel(flags_ref, f_ref, up_ref, down_ref, moved_ref):
    vel, gy = lax.axis_index("vel"), lax.axis_index("gy")
    subs, rows, lanes = iotas()
    own_rows = flag_tile(flags_ref, subs, gy)
    low_rows = flag_tile(flags_ref, subs, lax.rem(gy + 7, 8)).astype(F32)
    high_rows = flag_tile(flags_ref, subs, lax.rem(gy + 1, 8)).astype(F32)
    halo_rows = [pack_halo(r, r, rows, up) > 0.5 for r, up in ((high_rows, False), (low_rows, True))]

    def body(j, at, a_slot, right, up):
        speed_x, speed_y = speeds(vel, j)
        in_ref = up_ref if up else down_ref
        own = x_weights(speed_x, lanes, right, own_rows)
        out = x_weights(speed_x, lanes, right, halo_rows[up]) if right else own
        inflow = inflow_block(speed_x, speed_y) if right else None
        c0, c1, c2 = weights_of(speed_y)
        last = rows == (0 if up else 3)
        first = rows == (3 if up else 0)
        head = rows < 2 if up else rows >= 2
        s1, s2 = (1, 2) if up else (7, 6)
        own_base = own[3] * inflow if right else None
        out_base = out[3] * inflow if right else None
        for c in range(HALF):
            h = NV1 - 1 - c
            ghost = INFLOW_Z[c] * own_base if right else None
            low = sweep_x(f_ref[NV1 * j + c], own, right, ghost)
            high = sweep_x(f_ref[NV1 * j + h], own, right, ghost)
            halo = sweep_x(in_ref[at + c], out, right, INFLOW_Z[c] * out_base if right else None)
            low1 = pltpu.roll(jnp.where(first, halo, low), s1, 0)
            low2 = pltpu.roll(jnp.where(head, low, halo), s2, 0)
            high1 = jnp.where(last, pltpu.roll(halo, 8 - s1, 0), pltpu.roll(high, s1, 0))
            high2 = jnp.where(head, halo, pltpu.roll(high, s2, 0))
            moved_ref[NV1 * j + c] = c0 * low + c1 * low1 + c2 * low2
            moved_ref[NV1 * j + h] = c0 * high + c1 * high1 + c2 * high2

    over_blocks(vel, body)


def unpack_moments(own_ref, other_ref, vel, rows):
    odd = lax.rem(vel, 2) == 1
    low = rows < 2
    one, two = [], []
    for k in range(NPACK):
        a, b = own_ref[k], other_ref[k]
        upper, lower = jnp.where(odd, b, a), jnp.where(odd, a, b)
        one.append(jnp.where(low, upper, lower))
        two.append(jnp.where(low, pltpu.roll(upper, 6, 0), pltpu.roll(lower, 2, 0)))
    return (one + two)[:NMOM]


def cell_values(mom, solid):
    n = mom[0]
    inv = 1.0 / n
    ux, uy, uz = mom[1] * inv, mom[2] * inv, mom[3] * inv
    xx, yy, zz, xy, xz, yz = mom[4:10]
    energy = xx + yy + zz
    usq = ux * ux + uy * uy + uz * uz
    p = (energy - n * usq) * (1.0 / 3.0)
    common = 2.0 * n * usq - energy
    qx = 0.5 * (mom[10] - 2.0 * (xx * ux + xy * uy + xz * uz) + common * ux)
    qy = 0.5 * (mom[11] - 2.0 * (xy * ux + yy * uy + yz * uz) + common * uy)
    qz = 0.5 * (mom[12] - 2.0 * (xz * ux + yz * uy + zz * uz) + common * uz)
    temp = p * inv
    rate = p / (3000.0 * jnp.exp(0.81 * jnp.log(temp * (1.0 / 3.0))))
    damp = jnp.exp(-DT * rate)
    skew = (1.0 / 15.0) / (p * temp)
    zero = jnp.zeros(SHAPE, F32)
    n = jnp.where(solid, 200.0, n)
    temp = jnp.where(solid, 1.5, temp)
    damp = jnp.where(solid, zero, damp)
    skew = jnp.where(solid, zero, skew)
    ux, uy, uz = (jnp.where(solid, zero, u) for u in (ux, uy, uz))
    wide = 2.0 * math.pi * temp
    scale = n / (wide * jnp.sqrt(wide)) * (1.0 - damp)
    return scale, ux, uy, uz, 1.0 / temp, skew * qx, skew * qy, skew * qz, damp


def relax_kernel(last_step, flags_ref, mask_ref, own_ref, other_ref, moved_ref, *refs):
    if last_step:
        out_hbm, o_ref, z_ref, sems = refs
    else:
        o_ref, keep_ref, send_ref, up_ref, down_ref, acc_ref, z_ref = refs

    def o_copy(j):
        return pltpu.make_async_copy(o_ref.at[pl.ds(NV1 * j, NV1)], out_hbm.at[pl.ds(NV1 * j, NV1)], sems.at[j])

    vel, gy = lax.axis_index("vel"), lax.axis_index("gy")
    subs, rows, lanes = iotas()
    solid = mask_ref[...] > 0
    mom = unpack_moments(own_ref, other_ref, vel, rows)
    scale, ux, uy, uz, inv_t, qx, qy, qz, damp = cell_values(mom, solid)
    half_inv = -0.5 * inv_t
    for c in range(NV1):
        cz = ZS[c] - uz
        sq = cz * cz
        z_ref[c] = jnp.exp(sq * half_inv)
        z_ref[NV1 + c] = cz * qz
        z_ref[2 * NV1 + c] = sq * inv_t
    if not last_step:
        inflow_rows = flag_tile(flags_ref, subs, gy)
        clear_moments(acc_ref)

    def body(j, at, a_slot, right, up):
        speed_x, speed_y = speeds(vel, j)
        cx, cy = speed_x - ux, speed_y - uy
        sq = cx * cx + cy * cy
        e_xy = scale * jnp.exp(sq * half_inv)
        q_xy = cx * qx + cy * qy
        s_xy = sq * inv_t - 5.0

        def relax(c):
            shape = (q_xy + z_ref[NV1 + c]) * (s_xy + z_ref[2 * NV1 + c]) + 1.0
            return damp * moved_ref[NV1 * j + c] + (e_xy * z_ref[c]) * shape

        z = [jnp.zeros(SHAPE, F32)] * 4
        for c in range(HALF):
            h = NV1 - 1 - c
            low, high = relax(c), relax(h)
            o_ref[NV1 * j + c] = low
            o_ref[NV1 * j + h] = high
            if not last_step:
                z = z_sums(z, low, high, c)
                (up_ref if up else down_ref)[at + c] = pack_halo(low, high, rows, up)
        if last_step:
            o_copy(j).start()
        else:
            block_moments(acc_ref, a_slot, z, speed_x, speed_y, lanes, rows, right, up, inflow_rows)

    if last_step:
        lax.fori_loop(0, NB, lambda j, c: (body(j, 0, 0, True, True), c)[1], 0)
        for j in range(NB):
            o_copy(j).wait()
    else:
        over_blocks(vel, body)
        finish_moments(acc_ref, keep_ref, send_ref, vel, rows)


HBM = pl.BlockSpec(memory_space=pltpu.HBM)
SMEM = pl.BlockSpec(memory_space=pltpu.SMEM)
VMEM = pl.BlockSpec(memory_space=pltpu.VMEM)
SUMS = pltpu.VMEM((2 * NPACK, 8, 128), F32)
HALO = pltpu.VMEM((2 * SLOT, 8, 128), F32)
STATE = pltpu.VMEM((NB * NV1, 8, 128), F32)
ACC = pltpu.VMEM((4 * NORD, 8, 128), F32)
TABLE = pltpu.VMEM((3 * NV1, 8, 128), F32)
PARAMS = pltpu.CompilerParams(vmem_limit_bytes=12 << 20)
DMAS = pltpu.SemaphoreType.DMA((NB,))


def in_vmem(x):
    return pltpu.with_memory_space_constraint(x, pltpu.VMEM)


def first_call(flags, f):
    return pl.pallas_call(
        first_kernel,
        out_shape=(STATE, SUMS, SUMS, HALO, HALO),
        in_specs=[SMEM, HBM],
        out_specs=(VMEM,) * 5,
        scratch_shapes=[ACC, DMAS],
        compiler_params=PARAMS,
        name="first",
    )(flags, pltpu.with_memory_space_constraint(f, pltpu.HBM))


def move_call(flags, f, up, down):
    return pl.pallas_call(
        move_kernel,
        out_shape=STATE,
        in_specs=[SMEM, VMEM, VMEM, VMEM],
        out_specs=VMEM,
        compiler_params=PARAMS,
        name="move",
    )(flags, in_vmem(f), in_vmem(up), in_vmem(down))


def relax_call(last_step, flags, mask, own, other, moved):
    def kernel(*refs):
        relax_kernel(last_step, *refs)

    if last_step:
        out_shape = (jax.ShapeDtypeStruct(STATE.shape, F32),)
        out_specs, scratch, name = (HBM,), [STATE, TABLE, DMAS], "last"
    else:
        out_shape, out_specs = (STATE, SUMS, SUMS, HALO, HALO), (VMEM,) * 5
        scratch, name = [ACC, TABLE], "middle"
    return pl.pallas_call(
        kernel,
        out_shape=out_shape,
        in_specs=[SMEM, VMEM, VMEM, VMEM, VMEM],
        out_specs=out_specs,
        scratch_shapes=scratch,
        compiler_params=PARAMS,
        name=name,
    )(flags, mask, in_vmem(own), in_vmem(other), in_vmem(moved))


def shift(values, toward):
    pairs = [(v * 8 + g, v * 8 + (g + toward(v)) % 8) for v in range(32) for g in range(8)]
    return lax.ppermute(values, ("vel", "gy"), pairs)


def exchange(values, flip):
    return lax.ppermute(values, "vel", [(v, v ^ flip) for v in range(32)])


def tie(value, *others):
    return lax.optimization_barrier((value,) + others)[0]


def communicate(flags, f, keep, send, up, down):
    both = keep + exchange(send, 1)
    cross = shift(both[NPACK:], lambda v: 1 if v % 2 == 0 else -1)
    up = shift(tie(up, both), lambda v: 1)
    mom = both[:NPACK] + cross
    mom = mom + exchange(mom, 2)
    down = shift(tie(down, cross), lambda v: -1)
    mom = mom + exchange(mom, 6)
    mom = mom + exchange(mom, 8)
    moved = move_call(flags, f, tie(up, mom), tie(down, mom))
    mom = mom + exchange(mom, 24)
    return mom, exchange(mom, 1), moved


def shards(distribution, body_mask, inflow_flags):
    mask = body_mask.reshape(8, 128)
    parts = first_call(inflow_flags, distribution.reshape(NB * NV1, 8, 128))
    own, other, moved = communicate(inflow_flags, *parts)
    parts = relax_call(False, inflow_flags, mask, own, other, moved)
    own, other, moved = communicate(inflow_flags, *parts)
    (out,) = relax_call(True, inflow_flags, mask, own, other, moved)
    return out.reshape(distribution.shape)


def solution(mesh):
    placed = (P("vel", None, "gy", None), P(None, "gy", None), P())
    return jax.shard_map(
        shards, mesh=mesh, in_specs=placed, out_specs=P("vel", None, "gy", None), check_vma=False
    )
```

```python
import math

import jax
import jax.numpy as jnp
from jax import lax
from jax.experimental import pallas as pl
from jax.experimental.pallas import tpu as pltpu
from jax.sharding import PartitionSpec as P


NV1 = 24
NB = 18
HALF = NV1 // 2
NGROUP = 3
PER = NB // NGROUP
SLOT = PER * HALF
NMOM = 13
NPACK = 7
ORDERS = ((0, 0), (1, 0), (2, 0), (3, 0), (0, 1), (1, 1), (2, 1), (0, 2), (1, 2), (0, 3))
NORD = len(ORDERS)
STEP = 0.6
DT = 0.25
WEIGHT = STEP**3
CENTRE = 0.5 * (NV1 - 1)
ZS = [(c - CENTRE) * STEP for c in range(NV1)]
INFLOW_Z = [math.exp(-0.5 * z * z) for z in ZS]
INFLOW_SUMS = [sum(z**k * g for z, g in zip(ZS, INFLOW_Z)) for k in range(4)]
INFLOW_SCALE = 200.0 / (2.0 * math.pi) ** 1.5
SHAPE = (8, 128)
F32 = jnp.float32


def iotas():
    subs = lax.broadcasted_iota(jnp.int32, SHAPE, 0)
    lanes = lax.broadcasted_iota(jnp.int32, SHAPE, 1)
    return subs, jnp.bitwise_and(subs, 3), lanes


def flag_tile(flags_ref, subs, gy):
    tile = jnp.zeros(SHAPE, jnp.int32)
    for plane in range(2):
        for row in range(4):
            tile = jnp.where(subs == plane * 4 + row, flags_ref[plane, gy * 4 + row], tile)
    return tile > 0


def weights_of(speed):
    k = jnp.abs(speed) * DT
    return 1.0 - 1.5 * k + 0.5 * k * k, 2.0 * k - k * k, 0.5 * k * k - 0.5 * k


def speeds(vel, block):
    index = vel * NB + block
    a = lax.div(index, NV1)
    b = index - a * NV1
    return (a.astype(F32) - CENTRE) * STEP, (b.astype(F32) - CENTRE) * STEP


def group_state(vel, group):
    first = lax.rem(3 * vel, 4)

    def up_of(g):
        return lax.rem(first + g, 4) >= 2

    up = up_of(group)
    slot = jnp.where(jnp.logical_and(group > 0, up_of(0) == up), 1, 0)
    slot = slot + jnp.where(jnp.logical_and(group > 1, up_of(1) == up), 1, 0)
    a_slot = lax.div(vel * NB + PER * group, NV1) - lax.div(vel * NB, NV1)
    return up, slot, a_slot


def over_blocks(vel, body):
    for right in (True, False):

        @pl.when((vel >= 16) == right)
        def _(right=right):
            def group_loop(group, carry):
                up, slot, a_slot = group_state(vel, group)
                for up_now in (True, False):

                    @pl.when(up == up_now)
                    def _(up_now=up_now):
                        def block_loop(k, c):
                            body(PER * group + k, slot * SLOT + HALF * k, a_slot, right, up_now)
                            return c

                        lax.fori_loop(0, PER, block_loop, 0)

                return carry

            lax.fori_loop(0, NGROUP, group_loop, 0)


def inflow_block(speed_x, speed_y):
    drift = speed_x - 3.0
    return INFLOW_SCALE * jnp.exp(jnp.full(SHAPE, -0.5 * (drift * drift + speed_y * speed_y), F32))


def x_weights(speed_x, lanes, right, inflow_rows):
    c0, c1, c2 = weights_of(speed_x)
    zero = jnp.zeros(SHAPE, F32)
    v0, v1, v2 = (jnp.full(SHAPE, c, F32) for c in (c0, c1, c2))
    if right:
        edge, next_edge, inner = lanes == 0, lanes == 1, lanes >= 2
        held = jnp.logical_not(inflow_rows)
        a0 = jnp.where(jnp.logical_and(edge, held), 1.0, v0)
        a1 = jnp.where(edge, zero, jnp.where(jnp.logical_and(next_edge, held), v1 + v2, v1))
        a2 = jnp.where(inner, v2, zero)
        ghost = jnp.where(inflow_rows, jnp.where(edge, v1 + v2, jnp.where(next_edge, v2, zero)), zero)
        return a0, a1, a2, ghost
    edge, next_edge, inner = lanes == 127, lanes == 126, lanes < 126
    a0 = jnp.where(edge, 1.0, v0)
    a1 = jnp.where(edge, zero, jnp.where(next_edge, v1 + v2, v1))
    a2 = jnp.where(inner, v2, zero)
    return a0, a1, a2, None


def sweep_x(values, weights, right, ghost):
    one = pltpu.roll(values, 1 if right else 127, 1)
    two = pltpu.roll(values, 2 if right else 126, 1)
    swept = weights[0] * values + weights[1] * one + weights[2] * two
    return swept if ghost is None else swept + ghost


def z_sums(z, low, high, c):
    s = low + high
    d = high - low
    speed = ZS[NV1 - 1 - c]
    z0, z1, z2, z3 = z
    return [z0 + s, z1 + speed * d, z2 + speed**2 * s, z3 + speed**3 * d]


def pack_halo(low, high, rows, up):
    if up:
        return jnp.where(rows >= 2, pltpu.roll(low, 4, 0), pltpu.roll(high, 6, 0))
    return jnp.where(rows < 2, pltpu.roll(low, 4, 0), pltpu.roll(high, 2, 0))


def block_moments(acc_ref, a_slot, z, speed_x, speed_y, lanes, rows, right, up, inflow_rows):
    weights = x_weights(speed_x, lanes, right, inflow_rows)
    c0, c1, c2 = weights_of(speed_y)
    zero = jnp.zeros(SHAPE, F32)
    v1, v2 = jnp.full(SHAPE, c1, F32), jnp.full(SHAPE, c2, F32)
    last = rows == (0 if up else 3)
    head = rows < 2 if up else rows >= 2
    own1, cross1 = jnp.where(last, zero, v1), jnp.where(last, v1, zero)
    own2, cross2 = jnp.where(head, zero, v2), jnp.where(head, v2, zero)
    own, cross = [], []
    base = weights[3] * inflow_block(speed_x, speed_y) if right else None
    for k in range(4):
        ghost = INFLOW_SUMS[k] * base if right and k % 2 == 0 else None
        swept = sweep_x(z[k], weights, right, ghost)
        r1 = pltpu.roll(swept, 1 if up else 7, 0)
        r2 = pltpu.roll(swept, 2 if up else 6, 0)
        own.append(c0 * swept + own1 * r1 + own2 * r2)
        cross.append(cross1 * r1 + cross2 * r2)
    for side, values in enumerate((own, cross)):
        powers = {}
        for m, (j, k) in enumerate(ORDERS):
            powers[j, k] = values[k] if j == 0 else speed_y * powers[j - 1, k]
            at = a_slot * (2 * NORD) + side * NORD + m
            acc_ref[at] = acc_ref[at] + powers[j, k]


def clear_moments(acc_ref):
    for m in range(4 * NORD):
        acc_ref[m] = jnp.zeros(SHAPE, F32)


def finish_moments(acc_ref, keep_ref, send_ref, vel, rows):
    first_a = lax.div(vel * NB, NV1).astype(F32)
    odd = lax.rem(vel, 2) == 1
    low = rows < 2
    for side in range(2):
        total = None
        for a_slot in range(2):
            x = (first_a + (a_slot - CENTRE)) * STEP
            o = {jk: WEIGHT * acc_ref[a_slot * 2 * NORD + side * NORD + m] for m, jk in enumerate(ORDERS)}
            xo = x * o[0, 0]
            xx = x * xo
            terms = [
                o[0, 0], xo, o[1, 0], o[0, 1],
                xx, o[2, 0], o[0, 2],
                x * o[1, 0], x * o[0, 1], o[1, 1],
                x * xx + x * (o[2, 0] + o[0, 2]),
                x * x * o[1, 0] + (o[3, 0] + o[1, 2]),
                x * x * o[0, 1] + (o[2, 1] + o[0, 3]),
            ]
            total = terms if total is None else [p + q for p, q in zip(total, terms)]
        if side:
            total = [pltpu.roll(v, 4, 0) for v in total]
        for k in range(NPACK):
            one = total[k]
            two = total[k + NPACK] if k + NPACK < NMOM else one
            upper = jnp.where(low, one, pltpu.roll(two, 2, 0))
            lower = jnp.where(low, pltpu.roll(two, 6, 0), one)
            keep_ref[side * NPACK + k] = jnp.where(odd, lower, upper)
            send_ref[side * NPACK + k] = jnp.where(odd, upper, lower)


def first_kernel(flags_ref, f_hbm, f_ref, keep_ref, send_ref, up_ref, down_ref, acc_ref, sems):
    def f_copy(j):
        return pltpu.make_async_copy(f_hbm.at[pl.ds(NV1 * j, NV1)], f_ref.at[pl.ds(NV1 * j, NV1)], sems.at[j])

    for j in range(NB):
        f_copy(j).start()
    vel, gy = lax.axis_index("vel"), lax.axis_index("gy")
    subs, rows, lanes = iotas()
    inflow_rows = flag_tile(flags_ref, subs, gy)
    clear_moments(acc_ref)

    def body(j, at, a_slot, right, up):
        speed_x, speed_y = speeds(vel, j)
        out_ref = up_ref if up else down_ref
        f_copy(j).wait()
        z = [jnp.zeros(SHAPE, F32)] * 4
        for c in range(HALF):
            low = f_ref[NV1 * j + c]
            high = f_ref[NV1 * j + (NV1 - 1 - c)]
            z = z_sums(z, low, high, c)
            out_ref[at + c] = pack_halo(low, high, rows, up)
        block_moments(acc_ref, a_slot, z, speed_x, speed_y, lanes, rows, right, up, inflow_rows)

    over_blocks(vel, body)
    finish_moments(acc_ref, keep_ref, send_ref, vel, rows)


def move_kernel(flags_ref, f_ref, up_ref, down_ref, moved_ref):
    vel, gy = lax.axis_index("vel"), lax.axis_index("gy")
    subs, rows, lanes = iotas()
    own_rows = flag_tile(flags_ref, subs, gy)
    low_rows = flag_tile(flags_ref, subs, lax.rem(gy + 7, 8)).astype(F32)
    high_rows = flag_tile(flags_ref, subs, lax.rem(gy + 1, 8)).astype(F32)
    halo_rows = [pack_halo(r, r, rows, up) > 0.5 for r, up in ((high_rows, False), (low_rows, True))]

    def body(j, at, a_slot, right, up):
        speed_x, speed_y = speeds(vel, j)
        in_ref = up_ref if up else down_ref
        own = x_weights(speed_x, lanes, right, own_rows)
        out = x_weights(speed_x, lanes, right, halo_rows[up]) if right else own
        inflow = inflow_block(speed_x, speed_y) if right else None
        c0, c1, c2 = weights_of(speed_y)
        last = rows == (0 if up else 3)
        first = rows == (3 if up else 0)
        head = rows < 2 if up else rows >= 2
        s1, s2 = (1, 2) if up else (7, 6)
        own_base = own[3] * inflow if right else None
        out_base = out[3] * inflow if right else None
        for c in range(HALF):
            h = NV1 - 1 - c
            ghost = INFLOW_Z[c] * own_base if right else None
            low = sweep_x(f_ref[NV1 * j + c], own, right, ghost)
            high = sweep_x(f_ref[NV1 * j + h], own, right, ghost)
            halo = sweep_x(in_ref[at + c], out, right, INFLOW_Z[c] * out_base if right else None)
            low1 = pltpu.roll(jnp.where(first, halo, low), s1, 0)
            low2 = pltpu.roll(jnp.where(head, low, halo), s2, 0)
            high1 = jnp.where(last, pltpu.roll(halo, 8 - s1, 0), pltpu.roll(high, s1, 0))
            high2 = jnp.where(head, halo, pltpu.roll(high, s2, 0))
            moved_ref[NV1 * j + c] = c0 * low + c1 * low1 + c2 * low2
            moved_ref[NV1 * j + h] = c0 * high + c1 * high1 + c2 * high2

    over_blocks(vel, body)


def unpack_moments(own_ref, other_ref, vel, rows):
    odd = lax.rem(vel, 2) == 1
    low = rows < 2
    one, two = [], []
    for k in range(NPACK):
        a, b = own_ref[k], other_ref[k]
        upper, lower = jnp.where(odd, b, a), jnp.where(odd, a, b)
        one.append(jnp.where(low, upper, lower))
        two.append(jnp.where(low, pltpu.roll(upper, 6, 0), pltpu.roll(lower, 2, 0)))
    return (one + two)[:NMOM]


def cell_values(mom, solid):
    n = mom[0]
    inv = 1.0 / n
    ux, uy, uz = mom[1] * inv, mom[2] * inv, mom[3] * inv
    xx, yy, zz, xy, xz, yz = mom[4:10]
    energy = xx + yy + zz
    usq = ux * ux + uy * uy + uz * uz
    p = (energy - n * usq) * (1.0 / 3.0)
    common = 2.0 * n * usq - energy
    qx = 0.5 * (mom[10] - 2.0 * (xx * ux + xy * uy + xz * uz) + common * ux)
    qy = 0.5 * (mom[11] - 2.0 * (xy * ux + yy * uy + yz * uz) + common * uy)
    qz = 0.5 * (mom[12] - 2.0 * (xz * ux + yz * uy + zz * uz) + common * uz)
    temp = p * inv
    rate = p / (3000.0 * jnp.exp(0.81 * jnp.log(temp * (1.0 / 3.0))))
    damp = jnp.exp(-DT * rate)
    skew = (1.0 / 15.0) / (p * temp)
    zero = jnp.zeros(SHAPE, F32)
    n = jnp.where(solid, 200.0, n)
    temp = jnp.where(solid, 1.5, temp)
    damp = jnp.where(solid, zero, damp)
    skew = jnp.where(solid, zero, skew)
    ux, uy, uz = (jnp.where(solid, zero, u) for u in (ux, uy, uz))
    wide = 2.0 * math.pi * temp
    scale = n / (wide * jnp.sqrt(wide)) * (1.0 - damp)
    return scale, ux, uy, uz, 1.0 / temp, skew * qx, skew * qy, skew * qz, damp


def relax_kernel(last_step, flags_ref, mask_ref, own_ref, other_ref, moved_ref, *refs):
    if last_step:
        out_hbm, o_ref, z_ref, sems = refs
    else:
        o_ref, keep_ref, send_ref, up_ref, down_ref, acc_ref, z_ref = refs

    def o_copy(j):
        return pltpu.make_async_copy(o_ref.at[pl.ds(NV1 * j, NV1)], out_hbm.at[pl.ds(NV1 * j, NV1)], sems.at[j])

    vel, gy = lax.axis_index("vel"), lax.axis_index("gy")
    subs, rows, lanes = iotas()
    solid = mask_ref[...] > 0
    mom = unpack_moments(own_ref, other_ref, vel, rows)
    scale, ux, uy, uz, inv_t, qx, qy, qz, damp = cell_values(mom, solid)
    half_inv = -0.5 * inv_t
    for c in range(NV1):
        cz = ZS[c] - uz
        sq = cz * cz
        z_ref[c] = jnp.exp(sq * half_inv)
        z_ref[NV1 + c] = cz * qz
        z_ref[2 * NV1 + c] = sq * inv_t
    if not last_step:
        inflow_rows = flag_tile(flags_ref, subs, gy)
        clear_moments(acc_ref)

    def body(j, at, a_slot, right, up):
        speed_x, speed_y = speeds(vel, j)
        cx, cy = speed_x - ux, speed_y - uy
        sq = cx * cx + cy * cy
        e_xy = scale * jnp.exp(sq * half_inv)
        q_xy = cx * qx + cy * qy
        s_xy = sq * inv_t - 5.0

        def relax(c):
            shape = (q_xy + z_ref[NV1 + c]) * (s_xy + z_ref[2 * NV1 + c]) + 1.0
            return damp * moved_ref[NV1 * j + c] + (e_xy * z_ref[c]) * shape

        z = [jnp.zeros(SHAPE, F32)] * 4
        for c in range(HALF):
            h = NV1 - 1 - c
            low, high = relax(c), relax(h)
            o_ref[NV1 * j + c] = low
            o_ref[NV1 * j + h] = high
            if not last_step:
                z = z_sums(z, low, high, c)
                (up_ref if up else down_ref)[at + c] = pack_halo(low, high, rows, up)
        if last_step:
            o_copy(j).start()
        else:
            block_moments(acc_ref, a_slot, z, speed_x, speed_y, lanes, rows, right, up, inflow_rows)

    if last_step:
        lax.fori_loop(0, NB, lambda j, c: (body(j, 0, 0, True, True), c)[1], 0)
        for j in range(NB):
            o_copy(j).wait()
    else:
        over_blocks(vel, body)
        finish_moments(acc_ref, keep_ref, send_ref, vel, rows)


HBM = pl.BlockSpec(memory_space=pltpu.HBM)
SMEM = pl.BlockSpec(memory_space=pltpu.SMEM)
VMEM = pl.BlockSpec(memory_space=pltpu.VMEM)
SUMS = pltpu.VMEM((2 * NPACK, 8, 128), F32)
HALO = pltpu.VMEM((2 * SLOT, 8, 128), F32)
STATE = pltpu.VMEM((NB * NV1, 8, 128), F32)
ACC = pltpu.VMEM((4 * NORD, 8, 128), F32)
TABLE = pltpu.VMEM((3 * NV1, 8, 128), F32)
PARAMS = pltpu.CompilerParams(vmem_limit_bytes=12 << 20)
DMAS = pltpu.SemaphoreType.DMA((NB,))


def in_vmem(x):
    return pltpu.with_memory_space_constraint(x, pltpu.VMEM)


def first_call(flags, f):
    return pl.pallas_call(
        first_kernel,
        out_shape=(STATE, SUMS, SUMS, HALO, HALO),
        in_specs=[SMEM, HBM],
        out_specs=(VMEM,) * 5,
        scratch_shapes=[ACC, DMAS],
        compiler_params=PARAMS,
        name="first",
    )(pltpu.with_memory_space_constraint(flags, pltpu.HBM), pltpu.with_memory_space_constraint(f, pltpu.HBM))


def move_call(flags, f, up, down):
    return pl.pallas_call(
        move_kernel,
        out_shape=STATE,
        in_specs=[SMEM, VMEM, VMEM, VMEM],
        out_specs=VMEM,
        compiler_params=PARAMS,
        name="move",
    )(flags, in_vmem(f), in_vmem(up), in_vmem(down))


def relax_call(last_step, flags, mask, own, other, moved):
    def kernel(*refs):
        relax_kernel(last_step, *refs)

    if last_step:
        out_shape = (jax.ShapeDtypeStruct(STATE.shape, F32),)
        out_specs, scratch = (HBM,), [STATE, TABLE, DMAS]
    else:
        out_shape, out_specs = (STATE, SUMS, SUMS, HALO, HALO), (VMEM,) * 5
        scratch = [ACC, TABLE]
    return pl.pallas_call(
        kernel,
        out_shape=out_shape,
        in_specs=[SMEM, VMEM, VMEM, VMEM, VMEM],
        out_specs=out_specs,
        scratch_shapes=scratch,
        compiler_params=PARAMS,
    )(flags, mask, in_vmem(own), in_vmem(other), in_vmem(moved))


def permute(values, flip, z_shift=None):
    step = z_shift or (lambda v: 0)
    pairs = [(v * 8 + g, (v ^ flip) * 8 + (g + step(v)) % 8) for v in range(32) for g in range(8)]
    return lax.ppermute(values, ("vel", "gy"), pairs)


def tie(value, *others):
    return lax.optimization_barrier((value,) + others)[0]


def by_core(v):
    return 1 if v % 2 == 0 else -1


def communicate(flags, f, keep, send, up, down):
    both = keep + permute(send, 1)
    mom, cross = both[:NPACK], both[NPACK:]
    near = permute(mom, 2)
    side = permute(cross, 0, by_core)
    diagonal = permute(cross, 2, by_core)
    up = permute(tie(up, both), 0, lambda v: 1)
    down = permute(tie(down, both), 0, lambda v: -1)
    mom = (mom + near) + (side + diagonal)
    mom = mom + permute(mom, 6)
    first, second, third = (permute(mom, k) for k in (16, 8, 24))
    moved = move_call(flags, f, tie(up, mom), tie(down, mom))
    mom = (mom + second) + (first + third)
    return mom, permute(mom, 1), moved


def shards(distribution, body_mask, inflow_flags):
    mask = body_mask.reshape(8, 128)
    parts = first_call(inflow_flags, distribution.reshape(NB * NV1, 8, 128))
    own, other, moved = communicate(inflow_flags, *parts)
    parts = relax_call(False, inflow_flags, mask, own, other, moved)
    own, other, moved = communicate(inflow_flags, *parts)
    (out,) = relax_call(True, inflow_flags, mask, own, other, moved)
    return out.reshape(distribution.shape)


def solution(mesh):
    placed = (P("vel", None, "gy", None), P(None, "gy", None), P())
    return jax.shard_map(
        shards, mesh=mesh, in_specs=placed, out_specs=P("vel", None, "gy", None), check_vma=False
    )
```

```python
import math

import jax
import jax.numpy as jnp
from jax import lax
from jax.experimental import pallas as pl
from jax.experimental.pallas import tpu as pltpu
from jax.sharding import PartitionSpec as P


NV1 = 24
NB = 18
HALF = NV1 // 2
NGROUP = 3
PER = NB // NGROUP
SLOT = PER * HALF
NMOM = 13
NPACK = 7
ORDERS = ((0, 0), (1, 0), (2, 0), (3, 0), (0, 1), (1, 1), (2, 1), (0, 2), (1, 2), (0, 3))
NORD = len(ORDERS)
STEP = 0.6
DT = 0.25
WEIGHT = STEP**3
CENTRE = 0.5 * (NV1 - 1)
ZS = [(c - CENTRE) * STEP for c in range(NV1)]
INFLOW_Z = [math.exp(-0.5 * z * z) for z in ZS]
INFLOW_SUMS = [sum(z**k * g for z, g in zip(ZS, INFLOW_Z)) for k in range(4)]
INFLOW_SCALE = 200.0 / (2.0 * math.pi) ** 1.5
SHAPE = (8, 128)
F32 = jnp.float32


def iotas():
    subs = lax.broadcasted_iota(jnp.int32, SHAPE, 0)
    lanes = lax.broadcasted_iota(jnp.int32, SHAPE, 1)
    return subs, jnp.bitwise_and(subs, 3), lanes


def flag_tile(flags_ref, subs, gy):
    tile = jnp.zeros(SHAPE, F32)
    for plane in range(2):
        for row in range(4):
            value = flags_ref[plane, gy * 4 + row].astype(F32)
            tile = jnp.where(subs == plane * 4 + row, value, tile)
    return tile


def weights_of(speed):
    k = jnp.abs(speed) * DT
    return 1.0 - 1.5 * k + 0.5 * k * k, 2.0 * k - k * k, 0.5 * k * k - 0.5 * k


def speeds(vel, block):
    index = vel * NB + block
    a = lax.div(index, NV1)
    b = index - a * NV1
    return (a.astype(F32) - CENTRE) * STEP, (b.astype(F32) - CENTRE) * STEP


def group_state(vel, group):
    first = lax.rem(3 * vel, 4)

    def up_of(g):
        return lax.rem(first + g, 4) >= 2

    up = up_of(group)
    slot = jnp.where(jnp.logical_and(group > 0, up_of(0) == up), 1, 0)
    slot = slot + jnp.where(jnp.logical_and(group > 1, up_of(1) == up), 1, 0)
    a_slot = lax.div(vel * NB + PER * group, NV1) - lax.div(vel * NB, NV1)
    return up, slot, a_slot


def over_blocks(vel, body, ways=(True, False), by_right=True, finish=None):
    def groups(right):
        def group_loop(group, carry):
            up, slot, a_slot = group_state(vel, group)
            for up_now in ways:

                @pl.when(up == up_now)
                def _(up_now=up_now):
                    def block_loop(k, c):
                        body(PER * group + k, slot * SLOT + HALF * k, a_slot, right, up_now)
                        return c

                    lax.fori_loop(0, PER, block_loop, 0)
                    if finish is not None:
                        finish(group, a_slot, right, up_now)

            return carry

        lax.fori_loop(0, NGROUP, group_loop, 0)

    if not by_right:
        groups(None)
        return
    for right in (True, False):

        @pl.when((vel >= 16) == right)
        def _(right=right):
            groups(right)


def inflow_block(speed_x, speed_y):
    drift = speed_x - 3.0
    return INFLOW_SCALE * jnp.exp(jnp.full(SHAPE, -0.5 * (drift * drift + speed_y * speed_y), F32))


def x_weights(speed_x, lanes, right, inflow_rows):
    c0, c1, c2 = weights_of(speed_x)
    zero = jnp.zeros(SHAPE, F32)
    v0, v1, v2 = (jnp.full(SHAPE, c, F32) for c in (c0, c1, c2))
    if right:
        edge, next_edge, inner = lanes == 0, lanes == 1, lanes >= 2
        held = jnp.logical_not(inflow_rows)
        a0 = jnp.where(jnp.logical_and(edge, held), 1.0, v0)
        a1 = jnp.where(edge, zero, jnp.where(jnp.logical_and(next_edge, held), v1 + v2, v1))
        a2 = jnp.where(inner, v2, zero)
        ghost = jnp.where(inflow_rows, jnp.where(edge, v1 + v2, jnp.where(next_edge, v2, zero)), zero)
        return a0, a1, a2, ghost
    edge, next_edge, inner = lanes == 127, lanes == 126, lanes < 126
    a0 = jnp.where(edge, 1.0, v0)
    a1 = jnp.where(edge, zero, jnp.where(next_edge, v1 + v2, v1))
    a2 = jnp.where(inner, v2, zero)
    return a0, a1, a2, None


def sweep_x(values, weights, right, ghost):
    one = pltpu.roll(values, 1 if right else 127, 1)
    two = pltpu.roll(values, 2 if right else 126, 1)
    swept = weights[0] * values + weights[1] * one + weights[2] * two
    return swept if ghost is None else swept + ghost


def z_sums(z, low, high, c):
    s = low + high
    d = high - low
    speed = ZS[NV1 - 1 - c]
    z0, z1, z2, z3 = z
    return [z0 + s, z1 + speed * d, z2 + speed**2 * s, z3 + speed**3 * d]


def pack_halo(low, high, rows, up):
    if up:
        return jnp.where(rows >= 2, pltpu.roll(low, 4, 0), pltpu.roll(high, 6, 0))
    return jnp.where(rows < 2, pltpu.roll(low, 4, 0), pltpu.roll(high, 2, 0))


def group_moments(acc_ref, z_ref, vel, group, a_slot, lanes, rows, right, up, inflow_rows):
    last = rows == (0 if up else 3)
    head = rows < 2 if up else rows >= 2
    zero = jnp.zeros(SHAPE, F32)
    weights = x_weights(speeds(vel, PER * group)[0], lanes, right, inflow_rows)
    total = {}
    for n in range(PER):
        j = PER * group + n
        speed_x, speed_y = speeds(vel, j)
        c0, c1, c2 = weights_of(speed_y)
        v1, v2 = jnp.full(SHAPE, c1, F32), jnp.full(SHAPE, c2, F32)
        own1, cross1 = jnp.where(last, zero, v1), jnp.where(last, v1, zero)
        own2, cross2 = jnp.where(head, zero, v2), jnp.where(head, v2, zero)
        own, cross = [], []
        base = weights[3] * inflow_block(speed_x, speed_y) if right else None
        for k in range(4):
            ghost = INFLOW_SUMS[k] * base if right and k % 2 == 0 else None
            swept = sweep_x(z_ref[4 * j + k], weights, right, ghost)
            r1 = pltpu.roll(swept, 1 if up else 7, 0)
            r2 = pltpu.roll(swept, 2 if up else 6, 0)
            own.append(c0 * swept + own1 * r1 + own2 * r2)
            cross.append(cross1 * r1 + cross2 * r2)
        for side, values in enumerate((own, cross)):
            powers = {}
            for m, (i, k) in enumerate(ORDERS):
                powers[i, k] = values[k] if i == 0 else speed_y * powers[i - 1, k]
                at = side * NORD + m
                total[at] = total[at] + powers[i, k] if n else powers[i, k]
    for at, value in total.items():
        where = a_slot * (2 * NORD) + at
        acc_ref[where] = acc_ref[where] + value


def clear_moments(acc_ref):
    for m in range(4 * NORD):
        acc_ref[m] = jnp.zeros(SHAPE, F32)


def finish_moments(acc_ref, keep_ref, send_ref, vel, rows):
    first_a = lax.div(vel * NB, NV1).astype(F32)
    odd = lax.rem(vel, 2) == 1
    low = rows < 2
    for side in range(2):
        total = None
        for a_slot in range(2):
            x = (first_a + (a_slot - CENTRE)) * STEP
            o = {jk: WEIGHT * acc_ref[a_slot * 2 * NORD + side * NORD + m] for m, jk in enumerate(ORDERS)}
            xo = x * o[0, 0]
            xx = x * xo
            terms = [
                o[0, 0], xo, o[1, 0], o[0, 1],
                xx, o[2, 0], o[0, 2],
                x * o[1, 0], x * o[0, 1], o[1, 1],
                x * xx + x * (o[2, 0] + o[0, 2]),
                x * x * o[1, 0] + (o[3, 0] + o[1, 2]),
                x * x * o[0, 1] + (o[2, 1] + o[0, 3]),
            ]
            total = terms if total is None else [p + q for p, q in zip(total, terms)]
        if side:
            total = [pltpu.roll(v, 4, 0) for v in total]
        for k in range(NPACK):
            one = total[k]
            two = total[k + NPACK] if k + NPACK < NMOM else one
            upper = jnp.where(low, one, pltpu.roll(two, 2, 0))
            lower = jnp.where(low, pltpu.roll(two, 6, 0), one)
            keep_ref[side * NPACK + k] = jnp.where(odd, lower, upper)
            send_ref[side * NPACK + k] = jnp.where(odd, upper, lower)


def first_kernel(
    flags_hbm, f_hbm, f_ref, keep_ref, send_ref, up_ref, down_ref, tiles_ref, flags_ref, acc_ref, z_ref, sems, sem
):
    def f_copy(j):
        return pltpu.make_async_copy(f_hbm.at[pl.ds(NV1 * j, NV1)], f_ref.at[pl.ds(NV1 * j, NV1)], sems.at[j])

    flags_copy = pltpu.make_async_copy(flags_hbm, flags_ref, sem)
    flags_copy.start()
    for j in range(NB):
        f_copy(j).start()
    vel, gy = lax.axis_index("vel"), lax.axis_index("gy")
    subs, rows, lanes = iotas()
    clear_moments(acc_ref)
    flags_copy.wait()
    tiles_ref[0] = flag_tile(flags_ref, subs, gy)
    for at, turn, up in ((1, 7, True), (2, 1, False)):
        flags = flag_tile(flags_ref, subs, lax.rem(gy + turn, 8))
        tiles_ref[at] = pack_halo(flags, flags, rows, up)
    inflow_rows = tiles_ref[0] > 0.5

    def body(j, at, a_slot, right, up):
        out_ref = up_ref if up else down_ref
        f_copy(j).wait()
        z = [jnp.zeros(SHAPE, F32)] * 4
        for c in range(HALF):
            low = f_ref[NV1 * j + c]
            high = f_ref[NV1 * j + (NV1 - 1 - c)]
            z = z_sums(z, low, high, c)
            out_ref[at + c] = pack_halo(low, high, rows, up)
        for k in range(4):
            z_ref[4 * j + k] = z[k]

    def finish(group, a_slot, right, up):
        group_moments(acc_ref, z_ref, vel, group, a_slot, lanes, rows, right, up, inflow_rows)

    over_blocks(vel, body, finish=finish)
    finish_moments(acc_ref, keep_ref, send_ref, vel, rows)


def sweep_kernel(tiles_ref, f_ref, swept_ref):
    vel = lax.axis_index("vel")
    _, _, lanes = iotas()
    inflow_rows = tiles_ref[0] > 0.5
    for right in (True, False):

        @pl.when((vel >= 16) == right)
        def _(right=right):
            def block_loop(j, carry):
                speed_x, speed_y = speeds(vel, j)
                weights = x_weights(speed_x, lanes, right, inflow_rows)
                base = weights[3] * inflow_block(speed_x, speed_y) if right else None
                for c in range(HALF):
                    ghost = INFLOW_Z[c] * base if right else None
                    for v in (c, NV1 - 1 - c):
                        swept_ref[NV1 * j + v] = sweep_x(f_ref[NV1 * j + v], weights, right, ghost)
                return carry

            lax.fori_loop(0, NB, block_loop, 0)


def move_kernel(up, tiles_ref, swept_ref, halo_ref, moved_ref):
    vel = lax.axis_index("vel")
    _, rows, lanes = iotas()
    inflow_rows = tiles_ref[1 if up else 2] > 0.5
    last = rows == (0 if up else 3)
    first = rows == (3 if up else 0)
    head = rows < 2 if up else rows >= 2
    s1, s2 = (1, 2) if up else (7, 6)

    def body(j, at, a_slot, right, up):
        speed_x, speed_y = speeds(vel, j)
        weights = x_weights(speed_x, lanes, right, inflow_rows)
        base = weights[3] * inflow_block(speed_x, speed_y) if right else None
        c0, c1, c2 = weights_of(speed_y)
        for c in range(HALF):
            h = NV1 - 1 - c
            low, high = swept_ref[NV1 * j + c], swept_ref[NV1 * j + h]
            halo = sweep_x(halo_ref[at + c], weights, right, INFLOW_Z[c] * base if right else None)
            low1 = pltpu.roll(jnp.where(first, halo, low), s1, 0)
            low2 = pltpu.roll(jnp.where(head, low, halo), s2, 0)
            high1 = jnp.where(last, pltpu.roll(halo, 8 - s1, 0), pltpu.roll(high, s1, 0))
            high2 = jnp.where(head, halo, pltpu.roll(high, s2, 0))
            moved_ref[2 * at + c] = c0 * low + c1 * low1 + c2 * low2
            moved_ref[2 * at + h] = c0 * high + c1 * high1 + c2 * high2

    over_blocks(vel, body, (up,))


def unpack_moments(own_ref, other_ref, vel, rows):
    odd = lax.rem(vel, 2) == 1
    low = rows < 2
    one, two = [], []
    for k in range(NPACK):
        a, b = own_ref[k], other_ref[k]
        upper, lower = jnp.where(odd, b, a), jnp.where(odd, a, b)
        one.append(jnp.where(low, upper, lower))
        two.append(jnp.where(low, pltpu.roll(upper, 6, 0), pltpu.roll(lower, 2, 0)))
    return (one + two)[:NMOM]


def cell_values(mom, solid):
    n = mom[0]
    inv = 1.0 / n
    ux, uy, uz = mom[1] * inv, mom[2] * inv, mom[3] * inv
    xx, yy, zz, xy, xz, yz = mom[4:10]
    energy = xx + yy + zz
    usq = ux * ux + uy * uy + uz * uz
    p = (energy - n * usq) * (1.0 / 3.0)
    common = 2.0 * n * usq - energy
    qx = 0.5 * (mom[10] - 2.0 * (xx * ux + xy * uy + xz * uz) + common * ux)
    qy = 0.5 * (mom[11] - 2.0 * (xy * ux + yy * uy + yz * uz) + common * uy)
    qz = 0.5 * (mom[12] - 2.0 * (xz * ux + yz * uy + zz * uz) + common * uz)
    temp = p * inv
    rate = p / (3000.0 * jnp.exp(0.81 * jnp.log(temp * (1.0 / 3.0))))
    damp = jnp.exp(-DT * rate)
    skew = (1.0 / 15.0) / (p * temp)
    zero = jnp.zeros(SHAPE, F32)
    n = jnp.where(solid, 200.0, n)
    temp = jnp.where(solid, 1.5, temp)
    damp = jnp.where(solid, zero, damp)
    skew = jnp.where(solid, zero, skew)
    ux, uy, uz = (jnp.where(solid, zero, u) for u in (ux, uy, uz))
    wide = 2.0 * math.pi * temp
    scale = n / (wide * jnp.sqrt(wide)) * (1.0 - damp)
    return scale, ux, uy, uz, 1.0 / temp, skew * qx, skew * qy, skew * qz, damp


def relax_kernel(last_step, tiles_ref, mask_ref, own_ref, other_ref, up_moved_ref, down_moved_ref, *refs):
    if last_step:
        out_hbm, o_ref, z_ref, sems = refs
    else:
        o_ref, keep_ref, send_ref, up_ref, down_ref, acc_ref, zs_ref, z_ref = refs

    def o_copy(j):
        return pltpu.make_async_copy(o_ref.at[pl.ds(NV1 * j, NV1)], out_hbm.at[pl.ds(NV1 * j, NV1)], sems.at[j])

    vel = lax.axis_index("vel")
    _, rows, lanes = iotas()
    solid = mask_ref[...] > 0
    mom = unpack_moments(own_ref, other_ref, vel, rows)
    scale, ux, uy, uz, inv_t, qx, qy, qz, damp = cell_values(mom, solid)
    half_inv = -0.5 * inv_t
    for c in range(NV1):
        cz = ZS[c] - uz
        sq = cz * cz
        z_ref[c] = jnp.exp(sq * half_inv)
        z_ref[NV1 + c] = cz * qz
        z_ref[2 * NV1 + c] = sq * inv_t
    if not last_step:
        inflow_rows = tiles_ref[0] > 0.5
        clear_moments(acc_ref)

    def body(j, at, a_slot, right, up):
        speed_x, speed_y = speeds(vel, j)
        cx, cy = speed_x - ux, speed_y - uy
        sq = cx * cx + cy * cy
        e_xy = scale * jnp.exp(sq * half_inv)
        q_xy = cx * qx + cy * qy
        s_xy = sq * inv_t - 5.0

        moved_ref = up_moved_ref if up else down_moved_ref

        def relax(c):
            shape = (q_xy + z_ref[NV1 + c]) * (s_xy + z_ref[2 * NV1 + c]) + 1.0
            return damp * moved_ref[2 * at + c] + (e_xy * z_ref[c]) * shape

        z = [jnp.zeros(SHAPE, F32)] * 4
        for c in range(HALF):
            h = NV1 - 1 - c
            low, high = relax(c), relax(h)
            o_ref[NV1 * j + c] = low
            o_ref[NV1 * j + h] = high
            if not last_step:
                z = z_sums(z, low, high, c)
                (up_ref if up else down_ref)[at + c] = pack_halo(low, high, rows, up)
        if last_step:
            o_copy(j).start()
        else:
            for k in range(4):
                zs_ref[4 * j + k] = z[k]

    def finish(group, a_slot, right, up):
        group_moments(acc_ref, zs_ref, vel, group, a_slot, lanes, rows, right, up, inflow_rows)

    if last_step:
        over_blocks(vel, body, by_right=False)
        for j in range(NB):
            o_copy(j).wait()
    else:
        over_blocks(vel, body, finish=finish)
        finish_moments(acc_ref, keep_ref, send_ref, vel, rows)


HBM = pl.BlockSpec(memory_space=pltpu.HBM)
VMEM = pl.BlockSpec(memory_space=pltpu.VMEM)
SUMS = pltpu.VMEM((2 * NPACK, 8, 128), F32)
HALO = pltpu.VMEM((2 * SLOT, 8, 128), F32)
MOVED = pltpu.VMEM((4 * SLOT, 8, 128), F32)
STATE = pltpu.VMEM((NB * NV1, 8, 128), F32)
TILES = pltpu.VMEM((3, 8, 128), F32)
ZSUMS = pltpu.VMEM((4 * NB, 8, 128), F32)
ACC = pltpu.VMEM((4 * NORD, 8, 128), F32)
TABLE = pltpu.VMEM((3 * NV1, 8, 128), F32)
PARAMS = pltpu.CompilerParams(vmem_limit_bytes=12 << 20)
DMAS = pltpu.SemaphoreType.DMA((NB,))


def in_vmem(x):
    return pltpu.with_memory_space_constraint(x, pltpu.VMEM)


def first_call(flags, f):
    return pl.pallas_call(
        first_kernel,
        out_shape=(STATE, SUMS, SUMS, HALO, HALO, TILES),
        in_specs=[HBM, HBM],
        out_specs=(VMEM,) * 6,
        scratch_shapes=[pltpu.SMEM((2, 32), jnp.int32), ACC, ZSUMS, DMAS, pltpu.SemaphoreType.DMA(())],
        compiler_params=PARAMS,
        name="first",
    )(pltpu.with_memory_space_constraint(flags, pltpu.HBM), pltpu.with_memory_space_constraint(f, pltpu.HBM))


def sweep_call(tiles, f):
    return pl.pallas_call(
        sweep_kernel,
        out_shape=STATE,
        in_specs=[VMEM, VMEM],
        out_specs=VMEM,
        compiler_params=PARAMS,
        name="sweep",
    )(in_vmem(tiles), in_vmem(f))


def move_call(up, tiles, swept, halo):
    def kernel(*refs):
        move_kernel(up, *refs)

    return pl.pallas_call(
        kernel,
        out_shape=MOVED,
        in_specs=[VMEM, VMEM, VMEM],
        out_specs=VMEM,
        compiler_params=PARAMS,
        name="rise" if up else "fall",
    )(in_vmem(tiles), in_vmem(swept), in_vmem(halo))


def relax_call(last_step, tiles, mask, own, other, rise, fall):
    def kernel(*refs):
        relax_kernel(last_step, *refs)

    if last_step:
        out_shape = (jax.ShapeDtypeStruct(STATE.shape, F32),)
        out_specs, scratch = (HBM,), [STATE, TABLE, DMAS]
    else:
        out_shape, out_specs = (STATE, SUMS, SUMS, HALO, HALO), (VMEM,) * 5
        scratch = [ACC, ZSUMS, TABLE]
    return pl.pallas_call(
        kernel,
        out_shape=out_shape,
        in_specs=[VMEM] * 6,
        out_specs=out_specs,
        scratch_shapes=scratch,
        compiler_params=PARAMS,
    )(in_vmem(tiles), mask, in_vmem(own), in_vmem(other), in_vmem(rise), in_vmem(fall))


def permute(values, flip, z_shift=None):
    step = z_shift or (lambda v: 0)
    pairs = [(v * 8 + g, (v ^ flip) * 8 + (g + step(v)) % 8) for v in range(32) for g in range(8)]
    return lax.ppermute(values, ("vel", "gy"), pairs)


def tie(value, *others):
    return lax.optimization_barrier((value,) + others)[0]


def by_core(v):
    return 1 if v % 2 == 0 else -1


def communicate(tiles, f, keep, send, up, down):
    both = keep + permute(send, 1)
    mom, cross = both[:NPACK], both[NPACK:]
    near = permute(mom, 2)
    side = permute(cross, 0, by_core)
    diagonal = permute(cross, 2, by_core)
    up = permute(tie(up, both), 0, lambda v: 1)
    down = permute(tie(down, both), 0, lambda v: -1)
    mom = (mom + near) + (side + diagonal)
    swept = sweep_call(tiles, tie(f, mom))
    mom = mom + permute(mom, 6)
    first, second, third = (permute(mom, k) for k in (16, 8, 24))
    rise = move_call(True, tiles, swept, tie(up, mom))
    mom = (mom + second) + (first + third)
    fall = move_call(False, tiles, swept, tie(down, mom))
    return mom, permute(mom, 1), rise, fall


def shards(distribution, body_mask, inflow_flags):
    mask = body_mask.reshape(8, 128)
    *parts, tiles = first_call(inflow_flags, distribution.reshape(NB * NV1, 8, 128))
    parts = communicate(tiles, *parts)
    parts = relax_call(False, tiles, mask, *parts)
    parts = communicate(tiles, *parts)
    (out,) = relax_call(True, tiles, mask, *parts)
    return out.reshape(distribution.shape)


def solution(mesh):
    placed = (P("vel", None, "gy", None), P(None, "gy", None), P())
    return jax.shard_map(
        shards, mesh=mesh, in_specs=placed, out_specs=P("vel", None, "gy", None), check_vma=False
    )
```

```python
import math

import jax
import jax.numpy as jnp
from jax import lax
from jax.experimental import pallas as pl
from jax.experimental.pallas import tpu as pltpu
from jax.sharding import PartitionSpec as P


NV1 = 24
NB = 18
HALF = NV1 // 2
NGROUP = 3
PER = NB // NGROUP
SLOT = PER * HALF
NMOM = 13
NPACK = 7
ORDERS = ((0, 0), (1, 0), (2, 0), (3, 0), (0, 1), (1, 1), (2, 1), (0, 2), (1, 2), (0, 3))
NORD = len(ORDERS)
STEP = 0.6
DT = 0.25
WEIGHT = STEP**3
CENTRE = 0.5 * (NV1 - 1)
ZS = [(c - CENTRE) * STEP for c in range(NV1)]
INFLOW_Z = [math.exp(-0.5 * z * z) for z in ZS]
INFLOW_SUMS = [sum(z**k * g for z, g in zip(ZS, INFLOW_Z)) for k in range(4)]
INFLOW_SCALE = 200.0 / (2.0 * math.pi) ** 1.5
SHAPE = (8, 128)
F32 = jnp.float32


def iotas():
    subs = lax.broadcasted_iota(jnp.int32, SHAPE, 0)
    lanes = lax.broadcasted_iota(jnp.int32, SHAPE, 1)
    return subs, jnp.bitwise_and(subs, 3), lanes


def flag_tile(flags_ref, subs, gy):
    tile = jnp.zeros(SHAPE, F32)
    for plane in range(2):
        for row in range(4):
            value = flags_ref[plane, gy * 4 + row].astype(F32)
            tile = jnp.where(subs == plane * 4 + row, value, tile)
    return tile


def weights_of(speed):
    k = jnp.abs(speed) * DT
    return 1.0 - 1.5 * k + 0.5 * k * k, 2.0 * k - k * k, 0.5 * k * k - 0.5 * k


def speeds(vel, block):
    index = vel * NB + block
    a = lax.div(index, NV1)
    b = index - a * NV1
    return (a.astype(F32) - CENTRE) * STEP, (b.astype(F32) - CENTRE) * STEP


def group_state(vel, group):
    first = lax.rem(3 * vel, 4)

    def up_of(g):
        return lax.rem(first + g, 4) >= 2

    up = up_of(group)
    slot = jnp.where(jnp.logical_and(group > 0, up_of(0) == up), 1, 0)
    slot = slot + jnp.where(jnp.logical_and(group > 1, up_of(1) == up), 1, 0)
    a_slot = lax.div(vel * NB + PER * group, NV1) - lax.div(vel * NB, NV1)
    return up, slot, a_slot


def over_blocks(vel, body, ways=(True, False), by_right=True, finish=None):
    def groups(right):
        def group_loop(group, carry):
            up, slot, a_slot = group_state(vel, group)
            for up_now in ways:

                @pl.when(up == up_now)
                def _(up_now=up_now):
                    def block_loop(n, c):
                        for k in (3 * n, 3 * n + 1, 3 * n + 2):
                            body(PER * group + k, slot * SLOT + HALF * k, a_slot, right, up_now)
                        return c

                    lax.fori_loop(0, PER // 3, block_loop, 0)
                    if finish is not None:
                        finish(group, a_slot, right, up_now)

            return carry

        lax.fori_loop(0, NGROUP, group_loop, 0)

    if not by_right:
        groups(None)
        return
    for right in (True, False):

        @pl.when((vel >= 16) == right)
        def _(right=right):
            groups(right)


def inflow_block(speed_x, speed_y):
    drift = speed_x - 3.0
    return INFLOW_SCALE * jnp.exp(jnp.full(SHAPE, -0.5 * (drift * drift + speed_y * speed_y), F32))


def x_weights(speed_x, lanes, right, inflow_rows):
    c0, c1, c2 = weights_of(speed_x)
    zero = jnp.zeros(SHAPE, F32)
    v0, v1, v2 = (jnp.full(SHAPE, c, F32) for c in (c0, c1, c2))
    if right:
        edge, next_edge, inner = lanes == 0, lanes == 1, lanes >= 2
        held = jnp.logical_not(inflow_rows)
        a0 = jnp.where(jnp.logical_and(edge, held), 1.0, v0)
        a1 = jnp.where(edge, zero, jnp.where(jnp.logical_and(next_edge, held), v1 + v2, v1))
        a2 = jnp.where(inner, v2, zero)
        ghost = jnp.where(inflow_rows, jnp.where(edge, v1 + v2, jnp.where(next_edge, v2, zero)), zero)
        return a0, a1, a2, ghost
    edge, next_edge, inner = lanes == 127, lanes == 126, lanes < 126
    a0 = jnp.where(edge, 1.0, v0)
    a1 = jnp.where(edge, zero, jnp.where(next_edge, v1 + v2, v1))
    a2 = jnp.where(inner, v2, zero)
    return a0, a1, a2, None


def sweep_x(values, weights, right, ghost):
    one = pltpu.roll(values, 1 if right else 127, 1)
    two = pltpu.roll(values, 2 if right else 126, 1)
    swept = weights[0] * values + weights[1] * one + weights[2] * two
    return swept if ghost is None else swept + ghost


def z_sums(z, low, high, c):
    s = low + high
    d = high - low
    speed = ZS[NV1 - 1 - c]
    z0, z1, z2, z3 = z
    return [z0 + s, z1 + speed * d, z2 + speed**2 * s, z3 + speed**3 * d]


def pack_halo(low, high, rows, up):
    if up:
        return jnp.where(rows >= 2, pltpu.roll(low, 4, 0), pltpu.roll(high, 6, 0))
    return jnp.where(rows < 2, pltpu.roll(low, 4, 0), pltpu.roll(high, 2, 0))


def group_moments(acc_ref, z_ref, vel, group, a_slot, lanes, rows, right, up, inflow_rows):
    last = rows == (0 if up else 3)
    head = rows < 2 if up else rows >= 2
    zero = jnp.zeros(SHAPE, F32)
    weights = x_weights(speeds(vel, PER * group)[0], lanes, right, inflow_rows)
    total = {}
    for n in range(PER):
        j = PER * group + n
        speed_x, speed_y = speeds(vel, j)
        c0, c1, c2 = weights_of(speed_y)
        v1, v2 = jnp.full(SHAPE, c1, F32), jnp.full(SHAPE, c2, F32)
        own1, cross1 = jnp.where(last, zero, v1), jnp.where(last, v1, zero)
        own2, cross2 = jnp.where(head, zero, v2), jnp.where(head, v2, zero)
        own, cross = [], []
        base = weights[3] * inflow_block(speed_x, speed_y) if right else None
        for k in range(4):
            ghost = INFLOW_SUMS[k] * base if right and k % 2 == 0 else None
            swept = sweep_x(z_ref[4 * j + k], weights, right, ghost)
            r1 = pltpu.roll(swept, 1 if up else 7, 0)
            r2 = pltpu.roll(swept, 2 if up else 6, 0)
            own.append(c0 * swept + own1 * r1 + own2 * r2)
            cross.append(cross1 * r1 + cross2 * r2)
        for side, values in enumerate((own, cross)):
            powers = {}
            for m, (i, k) in enumerate(ORDERS):
                powers[i, k] = values[k] if i == 0 else speed_y * powers[i - 1, k]
                at = side * NORD + m
                total[at] = total[at] + powers[i, k] if n else powers[i, k]
    for at, value in total.items():
        where = a_slot * (2 * NORD) + at
        acc_ref[where] = acc_ref[where] + value


def clear_moments(acc_ref):
    for m in range(4 * NORD):
        acc_ref[m] = jnp.zeros(SHAPE, F32)


def finish_moments(acc_ref, keep_ref, send_ref, vel, rows):
    first_a = lax.div(vel * NB, NV1).astype(F32)
    odd = lax.rem(vel, 2) == 1
    low = rows < 2
    for side in range(2):
        total = None
        for a_slot in range(2):
            x = (first_a + (a_slot - CENTRE)) * STEP
            o = {jk: WEIGHT * acc_ref[a_slot * 2 * NORD + side * NORD + m] for m, jk in enumerate(ORDERS)}
            xo = x * o[0, 0]
            xx = x * xo
            terms = [
                o[0, 0], xo, o[1, 0], o[0, 1],
                xx, o[2, 0], o[0, 2],
                x * o[1, 0], x * o[0, 1], o[1, 1],
                x * xx + x * (o[2, 0] + o[0, 2]),
                x * x * o[1, 0] + (o[3, 0] + o[1, 2]),
                x * x * o[0, 1] + (o[2, 1] + o[0, 3]),
            ]
            total = terms if total is None else [p + q for p, q in zip(total, terms)]
        if side:
            total = [pltpu.roll(v, 4, 0) for v in total]
        for k in range(NPACK):
            one = total[k]
            two = total[k + NPACK] if k + NPACK < NMOM else one
            upper = jnp.where(low, one, pltpu.roll(two, 2, 0))
            lower = jnp.where(low, pltpu.roll(two, 6, 0), one)
            keep_ref[side * NPACK + k] = jnp.where(odd, lower, upper)
            send_ref[side * NPACK + k] = jnp.where(odd, upper, lower)


def first_kernel(
    flags_hbm, f_hbm, f_ref, keep_ref, send_ref, up_ref, down_ref, tiles_ref, flags_ref, acc_ref, z_ref, sems, sem
):
    def f_copy(j):
        return pltpu.make_async_copy(f_hbm.at[pl.ds(NV1 * j, NV1)], f_ref.at[pl.ds(NV1 * j, NV1)], sems.at[j])

    flags_copy = pltpu.make_async_copy(flags_hbm, flags_ref, sem)
    flags_copy.start()
    for j in range(NB):
        f_copy(j).start()
    vel, gy = lax.axis_index("vel"), lax.axis_index("gy")
    subs, rows, lanes = iotas()
    clear_moments(acc_ref)
    flags_copy.wait()
    tiles_ref[0] = flag_tile(flags_ref, subs, gy)
    for at, turn, up in ((1, 7, True), (2, 1, False)):
        flags = flag_tile(flags_ref, subs, lax.rem(gy + turn, 8))
        tiles_ref[at] = pack_halo(flags, flags, rows, up)
    inflow_rows = tiles_ref[0] > 0.5

    def body(j, at, a_slot, right, up):
        out_ref = up_ref if up else down_ref
        f_copy(j).wait()
        z = [jnp.zeros(SHAPE, F32)] * 4
        for c in range(HALF):
            low = f_ref[NV1 * j + c]
            high = f_ref[NV1 * j + (NV1 - 1 - c)]
            z = z_sums(z, low, high, c)
            out_ref[at + c] = pack_halo(low, high, rows, up)
        for k in range(4):
            z_ref[4 * j + k] = z[k]

    def finish(group, a_slot, right, up):
        group_moments(acc_ref, z_ref, vel, group, a_slot, lanes, rows, right, up, inflow_rows)

    over_blocks(vel, body, finish=finish)
    finish_moments(acc_ref, keep_ref, send_ref, vel, rows)


def sweep_kernel(tiles_ref, f_ref, swept_ref):
    vel = lax.axis_index("vel")
    _, _, lanes = iotas()
    inflow_rows = tiles_ref[0] > 0.5
    for right in (True, False):

        @pl.when((vel >= 16) == right)
        def _(right=right):
            def block_loop(j, carry):
                speed_x, speed_y = speeds(vel, j)
                weights = x_weights(speed_x, lanes, right, inflow_rows)
                base = weights[3] * inflow_block(speed_x, speed_y) if right else None
                for c in range(HALF):
                    ghost = INFLOW_Z[c] * base if right else None
                    for v in (c, NV1 - 1 - c):
                        swept_ref[NV1 * j + v] = sweep_x(f_ref[NV1 * j + v], weights, right, ghost)
                return carry

            lax.fori_loop(0, NB, block_loop, 0)


def move_kernel(up, tiles_ref, swept_ref, halo_ref, moved_ref):
    vel = lax.axis_index("vel")
    _, rows, lanes = iotas()
    inflow_rows = tiles_ref[1 if up else 2] > 0.5
    last = rows == (0 if up else 3)
    first = rows == (3 if up else 0)
    head = rows < 2 if up else rows >= 2
    s1, s2 = (1, 2) if up else (7, 6)

    def body(j, at, a_slot, right, up):
        speed_x, speed_y = speeds(vel, j)
        weights = x_weights(speed_x, lanes, right, inflow_rows)
        base = weights[3] * inflow_block(speed_x, speed_y) if right else None
        c0, c1, c2 = weights_of(speed_y)
        for c in range(HALF):
            h = NV1 - 1 - c
            low, high = swept_ref[NV1 * j + c], swept_ref[NV1 * j + h]
            halo = sweep_x(halo_ref[at + c], weights, right, INFLOW_Z[c] * base if right else None)
            low1 = pltpu.roll(jnp.where(first, halo, low), s1, 0)
            low2 = pltpu.roll(jnp.where(head, low, halo), s2, 0)
            high1 = jnp.where(last, pltpu.roll(halo, 8 - s1, 0), pltpu.roll(high, s1, 0))
            high2 = jnp.where(head, halo, pltpu.roll(high, s2, 0))
            moved_ref[2 * at + c] = c0 * low + c1 * low1 + c2 * low2
            moved_ref[2 * at + h] = c0 * high + c1 * high1 + c2 * high2

    over_blocks(vel, body, (up,))


def unpack_moments(own_ref, other_ref, vel, rows):
    odd = lax.rem(vel, 2) == 1
    low = rows < 2
    one, two = [], []
    for k in range(NPACK):
        a, b = own_ref[k], other_ref[k]
        upper, lower = jnp.where(odd, b, a), jnp.where(odd, a, b)
        one.append(jnp.where(low, upper, lower))
        two.append(jnp.where(low, pltpu.roll(upper, 6, 0), pltpu.roll(lower, 2, 0)))
    return (one + two)[:NMOM]


def cell_values(mom, solid):
    n = mom[0]
    inv = 1.0 / n
    ux, uy, uz = mom[1] * inv, mom[2] * inv, mom[3] * inv
    xx, yy, zz, xy, xz, yz = mom[4:10]
    energy = xx + yy + zz
    usq = ux * ux + uy * uy + uz * uz
    p = (energy - n * usq) * (1.0 / 3.0)
    common = 2.0 * n * usq - energy
    qx = 0.5 * (mom[10] - 2.0 * (xx * ux + xy * uy + xz * uz) + common * ux)
    qy = 0.5 * (mom[11] - 2.0 * (xy * ux + yy * uy + yz * uz) + common * uy)
    qz = 0.5 * (mom[12] - 2.0 * (xz * ux + yz * uy + zz * uz) + common * uz)
    temp = p * inv
    rate = p / (3000.0 * jnp.exp(0.81 * jnp.log(temp * (1.0 / 3.0))))
    damp = jnp.exp(-DT * rate)
    skew = (1.0 / 15.0) / (p * temp)
    zero = jnp.zeros(SHAPE, F32)
    n = jnp.where(solid, 200.0, n)
    temp = jnp.where(solid, 1.5, temp)
    damp = jnp.where(solid, zero, damp)
    skew = jnp.where(solid, zero, skew)
    ux, uy, uz = (jnp.where(solid, zero, u) for u in (ux, uy, uz))
    wide = 2.0 * math.pi * temp
    scale = n / (wide * jnp.sqrt(wide)) * (1.0 - damp)
    return scale, ux, uy, uz, 1.0 / temp, skew * qx, skew * qy, skew * qz, damp


def relax_kernel(last_step, tiles_ref, mask_ref, own_ref, other_ref, up_moved_ref, down_moved_ref, *refs):
    if last_step:
        out_hbm, o_ref, z_ref, sems = refs
    else:
        o_ref, keep_ref, send_ref, up_ref, down_ref, acc_ref, zs_ref, z_ref = refs

    def o_copy(j):
        return pltpu.make_async_copy(o_ref.at[pl.ds(NV1 * j, NV1)], out_hbm.at[pl.ds(NV1 * j, NV1)], sems.at[j])

    vel = lax.axis_index("vel")
    _, rows, lanes = iotas()
    solid = mask_ref[...] > 0
    mom = unpack_moments(own_ref, other_ref, vel, rows)
    scale, ux, uy, uz, inv_t, qx, qy, qz, damp = cell_values(mom, solid)
    half_inv = -0.5 * inv_t
    for c in range(NV1):
        cz = ZS[c] - uz
        sq = cz * cz
        z_ref[c] = jnp.exp(sq * half_inv)
        z_ref[NV1 + c] = cz * qz
        z_ref[2 * NV1 + c] = sq * inv_t
    if not last_step:
        inflow_rows = tiles_ref[0] > 0.5
        clear_moments(acc_ref)

    def body(j, at, a_slot, right, up):
        speed_x, speed_y = speeds(vel, j)
        cx, cy = speed_x - ux, speed_y - uy
        sq = cx * cx + cy * cy
        e_xy = scale * jnp.exp(sq * half_inv)
        q_xy = cx * qx + cy * qy
        s_xy = sq * inv_t - 5.0

        moved_ref = up_moved_ref if up else down_moved_ref

        def relax(c):
            shape = (q_xy + z_ref[NV1 + c]) * (s_xy + z_ref[2 * NV1 + c]) + 1.0
            return damp * moved_ref[2 * at + c] + (e_xy * z_ref[c]) * shape

        z = [jnp.zeros(SHAPE, F32)] * 4
        for c in range(HALF):
            h = NV1 - 1 - c
            low, high = relax(c), relax(h)
            o_ref[NV1 * j + c] = low
            o_ref[NV1 * j + h] = high
            if not last_step:
                z = z_sums(z, low, high, c)
                (up_ref if up else down_ref)[at + c] = pack_halo(low, high, rows, up)
        if last_step:
            o_copy(j).start()
        else:
            for k in range(4):
                zs_ref[4 * j + k] = z[k]

    def finish(group, a_slot, right, up):
        group_moments(acc_ref, zs_ref, vel, group, a_slot, lanes, rows, right, up, inflow_rows)

    if last_step:
        over_blocks(vel, body, by_right=False)
        for j in range(NB):
            o_copy(j).wait()
    else:
        over_blocks(vel, body, finish=finish)
        finish_moments(acc_ref, keep_ref, send_ref, vel, rows)


HBM = pl.BlockSpec(memory_space=pltpu.HBM)
VMEM = pl.BlockSpec(memory_space=pltpu.VMEM)
SUMS = pltpu.VMEM((2 * NPACK, 8, 128), F32)
HALO = pltpu.VMEM((2 * SLOT, 8, 128), F32)
MOVED = pltpu.VMEM((4 * SLOT, 8, 128), F32)
STATE = pltpu.VMEM((NB * NV1, 8, 128), F32)
TILES = pltpu.VMEM((3, 8, 128), F32)
ZSUMS = pltpu.VMEM((4 * NB, 8, 128), F32)
ACC = pltpu.VMEM((4 * NORD, 8, 128), F32)
TABLE = pltpu.VMEM((3 * NV1, 8, 128), F32)
PARAMS = pltpu.CompilerParams(vmem_limit_bytes=12 << 20)
DMAS = pltpu.SemaphoreType.DMA((NB,))


def in_vmem(x):
    return pltpu.with_memory_space_constraint(x, pltpu.VMEM)


def first_call(flags, f):
    return pl.pallas_call(
        first_kernel,
        out_shape=(STATE, SUMS, SUMS, HALO, HALO, TILES),
        in_specs=[HBM, HBM],
        out_specs=(VMEM,) * 6,
        scratch_shapes=[pltpu.SMEM((2, 32), jnp.int32), ACC, ZSUMS, DMAS, pltpu.SemaphoreType.DMA(())],
        compiler_params=PARAMS,
        name="first",
    )(pltpu.with_memory_space_constraint(flags, pltpu.HBM), pltpu.with_memory_space_constraint(f, pltpu.HBM))


def sweep_call(tiles, f):
    return pl.pallas_call(
        sweep_kernel,
        out_shape=STATE,
        in_specs=[VMEM, VMEM],
        out_specs=VMEM,
        compiler_params=PARAMS,
        name="sweep",
    )(in_vmem(tiles), in_vmem(f))


def move_call(up, tiles, swept, halo):
    def kernel(*refs):
        move_kernel(up, *refs)

    return pl.pallas_call(
        kernel,
        out_shape=MOVED,
        in_specs=[VMEM, VMEM, VMEM],
        out_specs=VMEM,
        compiler_params=PARAMS,
        name="rise" if up else "fall",
    )(in_vmem(tiles), in_vmem(swept), in_vmem(halo))


def relax_call(last_step, tiles, mask, own, other, rise, fall):
    def kernel(*refs):
        relax_kernel(last_step, *refs)

    if last_step:
        out_shape = (jax.ShapeDtypeStruct(STATE.shape, F32),)
        out_specs, scratch = (HBM,), [STATE, TABLE, DMAS]
    else:
        out_shape, out_specs = (STATE, SUMS, SUMS, HALO, HALO), (VMEM,) * 5
        scratch = [ACC, ZSUMS, TABLE]
    return pl.pallas_call(
        kernel,
        out_shape=out_shape,
        in_specs=[VMEM] * 6,
        out_specs=out_specs,
        scratch_shapes=scratch,
        compiler_params=PARAMS,
    )(in_vmem(tiles), mask, in_vmem(own), in_vmem(other), in_vmem(rise), in_vmem(fall))


def permute(values, flip, z_shift=None):
    step = z_shift or (lambda v: 0)
    pairs = [(v * 8 + g, (v ^ flip) * 8 + (g + step(v)) % 8) for v in range(32) for g in range(8)]
    return lax.ppermute(values, ("vel", "gy"), pairs)


def tie(value, *others):
    return lax.optimization_barrier((value,) + others)[0]


def by_core(v):
    return 1 if v % 2 == 0 else -1


def communicate(tiles, f, keep, send, up, down):
    both = keep + permute(send, 1)
    mom, cross = both[:NPACK], both[NPACK:]
    near = permute(mom, 8)
    side = permute(cross, 0, by_core)
    diagonal = permute(cross, 8, by_core)
    up = permute(tie(up, both), 0, lambda v: 1)
    down = permute(tie(down, both), 0, lambda v: -1)
    mom = (mom + near) + (side + diagonal)
    swept = sweep_call(tiles, tie(f, mom))
    mom = mom + permute(mom, 24)
    first, second, third = (permute(mom, k) for k in (4, 2, 6))
    rise = move_call(True, tiles, swept, tie(up, mom))
    mom = (mom + second) + (first + third)
    fall = move_call(False, tiles, swept, tie(down, mom))
    return mom, permute(mom, 1), rise, fall


def shards(distribution, body_mask, inflow_flags):
    mask = body_mask.reshape(8, 128)
    *parts, tiles = first_call(inflow_flags, distribution.reshape(NB * NV1, 8, 128))
    parts = communicate(tiles, *parts)
    parts = relax_call(False, tiles, mask, *parts)
    parts = communicate(tiles, *parts)
    (out,) = relax_call(True, tiles, mask, *parts)
    return out.reshape(distribution.shape)


def solution(mesh):
    placed = (P("vel", None, "gy", None), P(None, "gy", None), P())
    return jax.shard_map(
        shards, mesh=mesh, in_specs=placed, out_specs=P("vel", None, "gy", None), check_vma=False
    )
```

```python
import math

import jax
import jax.numpy as jnp
from jax import lax
from jax.experimental import pallas as pl
from jax.experimental.pallas import tpu as pltpu
from jax.sharding import PartitionSpec as P


NV1 = 24
NB = 18
HALF = NV1 // 2
NGROUP = 3
PER = NB // NGROUP
SLOT = PER * HALF
NMOM = 13
NPACK = 7
ORDERS = ((0, 0), (1, 0), (2, 0), (3, 0), (0, 1), (1, 1), (2, 1), (0, 2), (1, 2), (0, 3))
NORD = len(ORDERS)
STEP = 0.6
DT = 0.25
WEIGHT = STEP**3
CENTRE = 0.5 * (NV1 - 1)
ZS = [(c - CENTRE) * STEP for c in range(NV1)]
INFLOW_Z = [math.exp(-0.5 * z * z) for z in ZS]
INFLOW_SUMS = [sum(z**k * g for z, g in zip(ZS, INFLOW_Z)) for k in range(4)]
INFLOW_SCALE = 200.0 / (2.0 * math.pi) ** 1.5
SHAPE = (8, 128)
F32 = jnp.float32


def iotas():
    subs = lax.broadcasted_iota(jnp.int32, SHAPE, 0)
    lanes = lax.broadcasted_iota(jnp.int32, SHAPE, 1)
    return subs, jnp.bitwise_and(subs, 3), lanes


def flag_tile(flags_ref, subs, gy):
    tile = jnp.zeros(SHAPE, F32)
    for plane in range(2):
        for row in range(4):
            value = flags_ref[plane, gy * 4 + row].astype(F32)
            tile = jnp.where(subs == plane * 4 + row, value, tile)
    return tile


def weights_of(speed):
    k = jnp.abs(speed) * DT
    return 1.0 - 1.5 * k + 0.5 * k * k, 2.0 * k - k * k, 0.5 * k * k - 0.5 * k


def speeds(vel, block):
    index = vel * NB + block
    a = lax.div(index, NV1)
    b = index - a * NV1
    return (a.astype(F32) - CENTRE) * STEP, (b.astype(F32) - CENTRE) * STEP


def group_state(vel, group):
    first = lax.rem(3 * vel, 4)

    def up_of(g):
        return lax.rem(first + g, 4) >= 2

    up = up_of(group)
    slot = jnp.where(jnp.logical_and(group > 0, up_of(0) == up), 1, 0)
    slot = slot + jnp.where(jnp.logical_and(group > 1, up_of(1) == up), 1, 0)
    a_slot = lax.div(vel * NB + PER * group, NV1) - lax.div(vel * NB, NV1)
    return up, slot, a_slot


def over_blocks(vel, body, ways=(True, False), by_right=True, finish=None):
    def groups(right):
        def group_loop(group, carry):
            up, slot, a_slot = group_state(vel, group)
            for up_now in ways:

                @pl.when(up == up_now)
                def _(up_now=up_now):
                    def block_loop(c):
                        for k in range(PER):
                            body(PER * group + k, slot * SLOT + HALF * k, a_slot, right, up_now)
                        return c

                    block_loop(0)
                    if finish is not None:
                        finish(group, a_slot, right, up_now)

            return carry

        lax.fori_loop(0, NGROUP, group_loop, 0)

    if not by_right:
        groups(None)
        return
    for right in (True, False):

        @pl.when((vel >= 16) == right)
        def _(right=right):
            groups(right)


def inflow_block(speed_x, speed_y):
    drift = speed_x - 3.0
    return INFLOW_SCALE * jnp.exp(jnp.full(SHAPE, -0.5 * (drift * drift + speed_y * speed_y), F32))


def x_weights(speed_x, lanes, right, inflow_rows):
    c0, c1, c2 = weights_of(speed_x)
    zero = jnp.zeros(SHAPE, F32)
    v0, v1, v2 = (jnp.full(SHAPE, c, F32) for c in (c0, c1, c2))
    if right:
        edge, next_edge, inner = lanes == 0, lanes == 1, lanes >= 2
        held = jnp.logical_not(inflow_rows)
        a0 = jnp.where(jnp.logical_and(edge, held), 1.0, v0)
        a1 = jnp.where(edge, zero, jnp.where(jnp.logical_and(next_edge, held), v1 + v2, v1))
        a2 = jnp.where(inner, v2, zero)
        ghost = jnp.where(inflow_rows, jnp.where(edge, v1 + v2, jnp.where(next_edge, v2, zero)), zero)
        return a0, a1, a2, ghost
    edge, next_edge, inner = lanes == 127, lanes == 126, lanes < 126
    a0 = jnp.where(edge, 1.0, v0)
    a1 = jnp.where(edge, zero, jnp.where(next_edge, v1 + v2, v1))
    a2 = jnp.where(inner, v2, zero)
    return a0, a1, a2, None


def sweep_x(values, weights, right, ghost):
    one = pltpu.roll(values, 1 if right else 127, 1)
    two = pltpu.roll(values, 2 if right else 126, 1)
    swept = weights[0] * values + weights[1] * one + weights[2] * two
    return swept if ghost is None else swept + ghost


def z_sums(z, low, high, c):
    s = low + high
    d = high - low
    speed = ZS[NV1 - 1 - c]
    z0, z1, z2, z3 = z
    return [z0 + s, z1 + speed * d, z2 + speed**2 * s, z3 + speed**3 * d]


def pack_halo(low, high, rows, up):
    if up:
        return jnp.where(rows >= 2, pltpu.roll(low, 4, 0), pltpu.roll(high, 6, 0))
    return jnp.where(rows < 2, pltpu.roll(low, 4, 0), pltpu.roll(high, 2, 0))


def group_moments(acc_ref, z_ref, vel, group, a_slot, lanes, rows, right, up, inflow_rows):
    last = rows == (0 if up else 3)
    head = rows < 2 if up else rows >= 2
    zero = jnp.zeros(SHAPE, F32)
    weights = x_weights(speeds(vel, PER * group)[0], lanes, right, inflow_rows)
    total = {}
    for n in range(PER):
        j = PER * group + n
        speed_x, speed_y = speeds(vel, j)
        c0, c1, c2 = weights_of(speed_y)
        v1, v2 = jnp.full(SHAPE, c1, F32), jnp.full(SHAPE, c2, F32)
        own1, cross1 = jnp.where(last, zero, v1), jnp.where(last, v1, zero)
        own2, cross2 = jnp.where(head, zero, v2), jnp.where(head, v2, zero)
        own, cross = [], []
        base = weights[3] * inflow_block(speed_x, speed_y) if right else None
        for k in range(4):
            ghost = INFLOW_SUMS[k] * base if right and k % 2 == 0 else None
            swept = sweep_x(z_ref[4 * j + k], weights, right, ghost)
            r1 = pltpu.roll(swept, 1 if up else 7, 0)
            r2 = pltpu.roll(swept, 2 if up else 6, 0)
            own.append(c0 * swept + own1 * r1 + own2 * r2)
            cross.append(cross1 * r1 + cross2 * r2)
        for side, values in enumerate((own, cross)):
            powers = {}
            for m, (i, k) in enumerate(ORDERS):
                powers[i, k] = values[k] if i == 0 else speed_y * powers[i - 1, k]
                at = side * NORD + m
                total[at] = total[at] + powers[i, k] if n else powers[i, k]
    for at, value in total.items():
        where = a_slot * (2 * NORD) + at
        acc_ref[where] = acc_ref[where] + value


def clear_moments(acc_ref):
    for m in range(4 * NORD):
        acc_ref[m] = jnp.zeros(SHAPE, F32)


def finish_moments(acc_ref, keep_ref, send_ref, vel, rows):
    first_a = lax.div(vel * NB, NV1).astype(F32)
    odd = lax.rem(vel, 2) == 1
    low = rows < 2
    for side in range(2):
        total = None
        for a_slot in range(2):
            x = (first_a + (a_slot - CENTRE)) * STEP
            o = {jk: WEIGHT * acc_ref[a_slot * 2 * NORD + side * NORD + m] for m, jk in enumerate(ORDERS)}
            xo = x * o[0, 0]
            xx = x * xo
            terms = [
                o[0, 0], xo, o[1, 0], o[0, 1],
                xx, o[2, 0], o[0, 2],
                x * o[1, 0], x * o[0, 1], o[1, 1],
                x * xx + x * (o[2, 0] + o[0, 2]),
                x * x * o[1, 0] + (o[3, 0] + o[1, 2]),
                x * x * o[0, 1] + (o[2, 1] + o[0, 3]),
            ]
            total = terms if total is None else [p + q for p, q in zip(total, terms)]
        if side:
            total = [pltpu.roll(v, 4, 0) for v in total]
        for k in range(NPACK):
            one = total[k]
            two = total[k + NPACK] if k + NPACK < NMOM else one
            upper = jnp.where(low, one, pltpu.roll(two, 2, 0))
            lower = jnp.where(low, pltpu.roll(two, 6, 0), one)
            keep_ref[side * NPACK + k] = jnp.where(odd, lower, upper)
            send_ref[side * NPACK + k] = jnp.where(odd, upper, lower)


def first_kernel(
    flags_hbm, f_hbm, f_ref, keep_ref, send_ref, up_ref, down_ref, tiles_ref, flags_ref, acc_ref, z_ref, sems, sem
):
    def f_copy(j):
        return pltpu.make_async_copy(f_hbm.at[pl.ds(NV1 * j, NV1)], f_ref.at[pl.ds(NV1 * j, NV1)], sems.at[j])

    flags_copy = pltpu.make_async_copy(flags_hbm, flags_ref, sem)
    flags_copy.start()
    for j in range(NB):
        f_copy(j).start()
    vel, gy = lax.axis_index("vel"), lax.axis_index("gy")
    subs, rows, lanes = iotas()
    clear_moments(acc_ref)
    flags_copy.wait()
    tiles_ref[0] = flag_tile(flags_ref, subs, gy)
    for at, turn, up in ((1, 7, True), (2, 1, False)):
        flags = flag_tile(flags_ref, subs, lax.rem(gy + turn, 8))
        tiles_ref[at] = pack_halo(flags, flags, rows, up)
    inflow_rows = tiles_ref[0] > 0.5

    def body(j, at, a_slot, right, up):
        out_ref = up_ref if up else down_ref
        f_copy(j).wait()
        z = [jnp.zeros(SHAPE, F32)] * 4
        for c in range(HALF):
            low = f_ref[NV1 * j + c]
            high = f_ref[NV1 * j + (NV1 - 1 - c)]
            z = z_sums(z, low, high, c)
            out_ref[at + c] = pack_halo(low, high, rows, up)
        for k in range(4):
            z_ref[4 * j + k] = z[k]

    def finish(group, a_slot, right, up):
        group_moments(acc_ref, z_ref, vel, group, a_slot, lanes, rows, right, up, inflow_rows)

    over_blocks(vel, body, finish=finish)
    finish_moments(acc_ref, keep_ref, send_ref, vel, rows)


def sweep_kernel(tiles_ref, f_ref, swept_ref):
    vel = lax.axis_index("vel")
    _, _, lanes = iotas()
    inflow_rows = tiles_ref[0] > 0.5
    for right in (True, False):

        @pl.when((vel >= 16) == right)
        def _(right=right):
            def block_loop(j, carry):
                speed_x, speed_y = speeds(vel, j)
                weights = x_weights(speed_x, lanes, right, inflow_rows)
                base = weights[3] * inflow_block(speed_x, speed_y) if right else None
                for c in range(HALF):
                    ghost = INFLOW_Z[c] * base if right else None
                    for v in (c, NV1 - 1 - c):
                        swept_ref[NV1 * j + v] = sweep_x(f_ref[NV1 * j + v], weights, right, ghost)
                return carry

            lax.fori_loop(0, NB, block_loop, 0)


def move_kernel(up, tiles_ref, swept_ref, halo_ref, moved_ref):
    vel = lax.axis_index("vel")
    _, rows, lanes = iotas()
    inflow_rows = tiles_ref[1 if up else 2] > 0.5
    last = rows == (0 if up else 3)
    first = rows == (3 if up else 0)
    head = rows < 2 if up else rows >= 2
    s1, s2 = (1, 2) if up else (7, 6)

    def body(j, at, a_slot, right, up):
        speed_x, speed_y = speeds(vel, j)
        weights = x_weights(speed_x, lanes, right, inflow_rows)
        base = weights[3] * inflow_block(speed_x, speed_y) if right else None
        c0, c1, c2 = weights_of(speed_y)
        for c in range(HALF):
            h = NV1 - 1 - c
            low, high = swept_ref[NV1 * j + c], swept_ref[NV1 * j + h]
            halo = sweep_x(halo_ref[at + c], weights, right, INFLOW_Z[c] * base if right else None)
            low1 = pltpu.roll(jnp.where(first, halo, low), s1, 0)
            low2 = pltpu.roll(jnp.where(head, low, halo), s2, 0)
            high1 = jnp.where(last, pltpu.roll(halo, 8 - s1, 0), pltpu.roll(high, s1, 0))
            high2 = jnp.where(head, halo, pltpu.roll(high, s2, 0))
            moved_ref[2 * at + c] = c0 * low + c1 * low1 + c2 * low2
            moved_ref[2 * at + h] = c0 * high + c1 * high1 + c2 * high2

    over_blocks(vel, body, (up,))


def unpack_moments(own_ref, other_ref, vel, rows):
    odd = lax.rem(vel, 2) == 1
    low = rows < 2
    one, two = [], []
    for k in range(NPACK):
        a, b = own_ref[k], other_ref[k]
        upper, lower = jnp.where(odd, b, a), jnp.where(odd, a, b)
        one.append(jnp.where(low, upper, lower))
        two.append(jnp.where(low, pltpu.roll(upper, 6, 0), pltpu.roll(lower, 2, 0)))
    return (one + two)[:NMOM]


def cell_values(mom, solid):
    n = mom[0]
    inv = 1.0 / n
    ux, uy, uz = mom[1] * inv, mom[2] * inv, mom[3] * inv
    xx, yy, zz, xy, xz, yz = mom[4:10]
    energy = xx + yy + zz
    usq = ux * ux + uy * uy + uz * uz
    p = (energy - n * usq) * (1.0 / 3.0)
    common = 2.0 * n * usq - energy
    qx = 0.5 * (mom[10] - 2.0 * (xx * ux + xy * uy + xz * uz) + common * ux)
    qy = 0.5 * (mom[11] - 2.0 * (xy * ux + yy * uy + yz * uz) + common * uy)
    qz = 0.5 * (mom[12] - 2.0 * (xz * ux + yz * uy + zz * uz) + common * uz)
    temp = p * inv
    rate = p / (3000.0 * jnp.exp(0.81 * jnp.log(temp * (1.0 / 3.0))))
    damp = jnp.exp(-DT * rate)
    skew = (1.0 / 15.0) / (p * temp)
    zero = jnp.zeros(SHAPE, F32)
    n = jnp.where(solid, 200.0, n)
    temp = jnp.where(solid, 1.5, temp)
    damp = jnp.where(solid, zero, damp)
    skew = jnp.where(solid, zero, skew)
    ux, uy, uz = (jnp.where(solid, zero, u) for u in (ux, uy, uz))
    wide = 2.0 * math.pi * temp
    scale = n / (wide * jnp.sqrt(wide)) * (1.0 - damp)
    return scale, ux, uy, uz, 1.0 / temp, skew * qx, skew * qy, skew * qz, damp


def relax_kernel(last_step, tiles_ref, mask_ref, own_ref, other_ref, up_moved_ref, down_moved_ref, *refs):
    if last_step:
        out_hbm, o_ref, z_ref, sems = refs
    else:
        o_ref, keep_ref, send_ref, up_ref, down_ref, acc_ref, zs_ref, z_ref = refs

    def o_copy(j):
        return pltpu.make_async_copy(o_ref.at[pl.ds(NV1 * j, NV1)], out_hbm.at[pl.ds(NV1 * j, NV1)], sems.at[j])

    vel = lax.axis_index("vel")
    _, rows, lanes = iotas()
    solid = mask_ref[...] > 0
    mom = unpack_moments(own_ref, other_ref, vel, rows)
    scale, ux, uy, uz, inv_t, qx, qy, qz, damp = cell_values(mom, solid)
    half_inv = -0.5 * inv_t
    for c in range(NV1):
        cz = ZS[c] - uz
        sq = cz * cz
        z_ref[c] = jnp.exp(sq * half_inv)
        z_ref[NV1 + c] = cz * qz
        z_ref[2 * NV1 + c] = sq * inv_t
    if not last_step:
        inflow_rows = tiles_ref[0] > 0.5
        clear_moments(acc_ref)

    def body(j, at, a_slot, right, up):
        speed_x, speed_y = speeds(vel, j)
        cx, cy = speed_x - ux, speed_y - uy
        sq = cx * cx + cy * cy
        e_xy = scale * jnp.exp(sq * half_inv)
        q_xy = cx * qx + cy * qy
        s_xy = sq * inv_t - 5.0

        moved_ref = up_moved_ref if up else down_moved_ref

        def relax(c):
            shape = (q_xy + z_ref[NV1 + c]) * (s_xy + z_ref[2 * NV1 + c]) + 1.0
            return damp * moved_ref[2 * at + c] + (e_xy * z_ref[c]) * shape

        z = [jnp.zeros(SHAPE, F32)] * 4
        for c in range(HALF):
            h = NV1 - 1 - c
            low, high = relax(c), relax(h)
            o_ref[NV1 * j + c] = low
            o_ref[NV1 * j + h] = high
            if not last_step:
                z = z_sums(z, low, high, c)
                (up_ref if up else down_ref)[at + c] = pack_halo(low, high, rows, up)
        if last_step:
            o_copy(j).start()
        else:
            for k in range(4):
                zs_ref[4 * j + k] = z[k]

    def finish(group, a_slot, right, up):
        group_moments(acc_ref, zs_ref, vel, group, a_slot, lanes, rows, right, up, inflow_rows)

    if last_step:
        over_blocks(vel, body, by_right=False)
        for j in range(NB):
            o_copy(j).wait()
    else:
        over_blocks(vel, body, finish=finish)
        finish_moments(acc_ref, keep_ref, send_ref, vel, rows)


HBM = pl.BlockSpec(memory_space=pltpu.HBM)
VMEM = pl.BlockSpec(memory_space=pltpu.VMEM)
SUMS = pltpu.VMEM((2 * NPACK, 8, 128), F32)
HALO = pltpu.VMEM((2 * SLOT, 8, 128), F32)
MOVED = pltpu.VMEM((4 * SLOT, 8, 128), F32)
STATE = pltpu.VMEM((NB * NV1, 8, 128), F32)
TILES = pltpu.VMEM((3, 8, 128), F32)
ZSUMS = pltpu.VMEM((4 * NB, 8, 128), F32)
ACC = pltpu.VMEM((4 * NORD, 8, 128), F32)
TABLE = pltpu.VMEM((3 * NV1, 8, 128), F32)
PARAMS = pltpu.CompilerParams(vmem_limit_bytes=12 << 20)
DMAS = pltpu.SemaphoreType.DMA((NB,))


def in_vmem(x):
    return pltpu.with_memory_space_constraint(x, pltpu.VMEM)


def first_call(flags, f):
    return pl.pallas_call(
        first_kernel,
        out_shape=(STATE, SUMS, SUMS, HALO, HALO, TILES),
        in_specs=[HBM, HBM],
        out_specs=(VMEM,) * 6,
        scratch_shapes=[pltpu.SMEM((2, 32), jnp.int32), ACC, ZSUMS, DMAS, pltpu.SemaphoreType.DMA(())],
        compiler_params=PARAMS,
        name="first",
    )(pltpu.with_memory_space_constraint(flags, pltpu.HBM), pltpu.with_memory_space_constraint(f, pltpu.HBM))


def sweep_call(tiles, f):
    return pl.pallas_call(
        sweep_kernel,
        out_shape=STATE,
        in_specs=[VMEM, VMEM],
        out_specs=VMEM,
        compiler_params=PARAMS,
        name="sweep",
    )(in_vmem(tiles), in_vmem(f))


def move_call(up, tiles, swept, halo):
    def kernel(*refs):
        move_kernel(up, *refs)

    return pl.pallas_call(
        kernel,
        out_shape=MOVED,
        in_specs=[VMEM, VMEM, VMEM],
        out_specs=VMEM,
        compiler_params=PARAMS,
        name="rise" if up else "fall",
    )(in_vmem(tiles), in_vmem(swept), in_vmem(halo))


def relax_call(last_step, tiles, mask, own, other, rise, fall):
    def kernel(*refs):
        relax_kernel(last_step, *refs)

    if last_step:
        out_shape = (jax.ShapeDtypeStruct(STATE.shape, F32),)
        out_specs, scratch = (HBM,), [STATE, TABLE, DMAS]
    else:
        out_shape, out_specs = (STATE, SUMS, SUMS, HALO, HALO), (VMEM,) * 5
        scratch = [ACC, ZSUMS, TABLE]
    return pl.pallas_call(
        kernel,
        out_shape=out_shape,
        in_specs=[VMEM] * 6,
        out_specs=out_specs,
        scratch_shapes=scratch,
        compiler_params=PARAMS,
    )(in_vmem(tiles), mask, in_vmem(own), in_vmem(other), in_vmem(rise), in_vmem(fall))


def permute(values, flip, z_shift=None):
    step = z_shift or (lambda v: 0)
    pairs = [(v * 8 + g, (v ^ flip) * 8 + (g + step(v)) % 8) for v in range(32) for g in range(8)]
    return lax.ppermute(values, ("vel", "gy"), pairs)


def tie(value, *others):
    return lax.optimization_barrier((value,) + others)[0]


def by_core(v):
    return 1 if v % 2 == 0 else -1


def communicate(tiles, f, keep, send, up, down):
    both = keep + permute(send, 1)
    mom, cross = both[:NPACK], both[NPACK:]
    near = permute(mom, 8)
    side = permute(cross, 0, by_core)
    diagonal = permute(cross, 8, by_core)
    up = permute(tie(up, both), 0, lambda v: 1)
    down = permute(tie(down, both), 0, lambda v: -1)
    mom = (mom + near) + (side + diagonal)
    swept = sweep_call(tiles, tie(f, mom))
    mom = mom + permute(mom, 24)
    first, second, third = (permute(mom, k) for k in (4, 2, 6))
    rise = move_call(True, tiles, swept, tie(up, mom))
    mom = (mom + second) + (first + third)
    fall = move_call(False, tiles, swept, tie(down, mom))
    return mom, permute(mom, 1), rise, fall


def shards(distribution, body_mask, inflow_flags):
    mask = body_mask.reshape(8, 128)
    *parts, tiles = first_call(inflow_flags, distribution.reshape(NB * NV1, 8, 128))
    parts = communicate(tiles, *parts)
    parts = relax_call(False, tiles, mask, *parts)
    parts = communicate(tiles, *parts)
    (out,) = relax_call(True, tiles, mask, *parts)
    return out.reshape(distribution.shape)


def solution(mesh):
    placed = (P("vel", None, "gy", None), P(None, "gy", None), P())
    return jax.shard_map(
        shards, mesh=mesh, in_specs=placed, out_specs=P("vel", None, "gy", None), check_vma=False
    )
```
